32 devices in a mesh: crops: 1, rows: 16 (over z, y, core), cols: 2 (over x).
Axes of the slice: x: 2, y: 2, z: 4, core: 2. Of those that a mesh axis runs over, the one named last changes fastest.
Arguments:
- family_representation: float32 [128, 256, 256], P(('crops', 'rows'), 'cols'), may hold values from -6 to 6
- family_keep_flags: int32 [128, 256], P(('crops', 'rows'), 'cols'), may hold values 0 or 1
- amino_presence: int32 [256], P('crops'), may hold values 0 or 1
- contact_embedding: float32 [256, 256, 128], P(('crops', 'rows'), 'cols'), may hold values from -6 to 6
- couple_lhs_weights: bfloat16 [256, 32], replicated, may hold values from -0.375 to 0.375
- couple_rhs_weights: bfloat16 [256, 32], replicated, may hold values from -0.375 to 0.375
- pairwise_final_matrix: bfloat16 [1024, 128], replicated, may hold values from -1.5 to 1.5
- edge_source_matrix: bfloat16 [128, 256], replicated, may hold values from -0.5 to 0.5
- edge_target_matrix: bfloat16 [128, 256], replicated, may hold values from -0.5 to 0.5
- edge_final_sigmoid_matrix: bfloat16 [128, 128], replicated, may hold values from -0.5 to 0.5
- edge_final_matrix: bfloat16 [128, 128], replicated, may hold values from -0.5 to 0.5
- feedforward_expand_matrix: bfloat16 [128, 512], replicated, may hold values from -0.5 to 0.5
- feedforward_shrink_matrix: bfloat16 [512, 128], replicated, may hold values from -0.25 to 0.25
Outputs:
- pair_out: float32 [256, 256, 128], P(('crops', 'rows'), 'cols')
The draws below stay inside these ranges and needn't reach their ends.
All inputs are finite; a program needn't handle non-finite values. No bound on the sum of `family_keep_flags` on one device may be relied on, other than what follows from the above.
Results may differ from the reference program's by a relative error of at most 0.0053.
Values may be sent and summed in bfloat16 or wider, within the bound.
A program may use at most 64 MiB of HBM per device.

```python
import jax
import jax.numpy as jnp
from jax import lax

FAMILY_FEATS = 256
OPM_CHANS = 32
CZ = 128
CT = 128
CH = 512
FAMILY_ENTRIES = 128
CRAFT_SPAN = 256


def set_ends(drawn, rng, low, high):
    place = [jax.random.randint(jax.random.fold_in(rng, axis), (), 0, length) for axis, length in enumerate(drawn.shape)]
    main_axis = drawn.shape.index(max(drawn.shape))
    neighbour = place[:main_axis] + [(place[main_axis] + 1) % drawn.shape[main_axis]] + place[main_axis + 1:]
    return drawn.at[tuple(place)].set(low).at[tuple(neighbour)].set(high)


def level_of(key, extent, pieces, least, top_value):
    gain, own = 1.0, jax.random.fold_in(key, 6)
    for position, shards_of in pieces:
        draws = jnp.exp(jax.random.uniform(jax.random.fold_in(own, position), (shards_of,), jnp.float32, least / len(pieces), top_value / len(pieces)))
        gain = gain * jnp.repeat(draws, extent[position] // shards_of).reshape([-1 if axis == position else 1 for axis in range(len(extent))])
    return gain


def gaussian(own_key, shape, scale, reach, cuts=(), held_as=jnp.bfloat16):
    loudness = level_of(own_key, shape, cuts, -0.22, 0.18) if cuts else 1.0
    values = jax.random.normal(own_key, shape, jnp.float32) * scale * loudness
    return jnp.minimum(jnp.maximum(values, -reach), reach).astype(held_as)


def setup_inputs(seed: int = 0, part: int = 0) -> dict:
    key_of = jax.random.split(jax.random.key(seed), 14)
    part_splits = jax.random.split(jax.random.fold_in(key_of[13], part), 14)
    return {
        "family_representation": gaussian(part_splits[0], (FAMILY_ENTRIES, CRAFT_SPAN, FAMILY_FEATS), 1.0, 6.0, ((0, 16), (1, 2)), jnp.float32),
        "family_keep_flags": set_ends((jax.random.randint(part_splits[1], (FAMILY_ENTRIES, CRAFT_SPAN), 0, 4) < 3).astype(jnp.int32), jax.random.fold_in(part_splits[1], 1), 0, 1),
        "amino_presence": set_ends((jax.random.randint(part_splits[2], (CRAFT_SPAN,), 0, 16) < 15).astype(jnp.int32), jax.random.fold_in(part_splits[2], 1), 0, 1),
        "contact_embedding": gaussian(part_splits[3], (CRAFT_SPAN, CRAFT_SPAN, CZ), 1.0, 6.0, ((0, 16), (1, 2)), jnp.float32),
        "couple_lhs_weights": gaussian(key_of[4], (FAMILY_FEATS, OPM_CHANS), FAMILY_FEATS ** -0.5, 0.375),
        "couple_rhs_weights": gaussian(key_of[5], (FAMILY_FEATS, OPM_CHANS), FAMILY_FEATS ** -0.5, 0.375),
        "pairwise_final_matrix": gaussian(key_of[6], (OPM_CHANS * OPM_CHANS, CZ), (OPM_CHANS * OPM_CHANS // 64) ** -0.5, 1.5),
        "edge_source_matrix": gaussian(key_of[7], (CZ, 2 * CT), CZ ** -0.5, 0.5),
        "edge_target_matrix": gaussian(key_of[8], (CZ, 2 * CT), CZ ** -0.5, 0.5),
        "edge_final_sigmoid_matrix": gaussian(key_of[9], (CZ, CZ), CZ ** -0.5, 0.5),
        "edge_final_matrix": gaussian(key_of[10], (CT, CZ), CT ** -0.5, 0.5),
        "feedforward_expand_matrix": gaussian(key_of[11], (CZ, CH), CZ ** -0.5, 0.5),
        "feedforward_shrink_matrix": gaussian(key_of[12], (CH, CZ), CH ** -0.5, 0.25),
    }


epsilon = 1e-05

def normalise_features_step(values, reduce_axis):
    mean = lax.optimization_barrier(jnp.mean(values, axis=reduce_axis, keepdims=True))
    centred = values - mean
    spread = lax.optimization_barrier(jnp.mean(centred * centred, axis=reduce_axis, keepdims=True))
    return centred * lax.rsqrt(spread + epsilon)

def reduced_numeric_kind(values):
    return lax.optimization_barrier(values.astype(jnp.bfloat16)).astype(jnp.float32)

def growth_multiple(values):
    return values.astype(jnp.float32)

def reference(family_representation, family_keep_flags, amino_presence, contact_embedding, couple_lhs_weights, couple_rhs_weights, pairwise_final_matrix, edge_source_matrix, edge_target_matrix, edge_final_sigmoid_matrix, edge_final_matrix, feedforward_expand_matrix, feedforward_shrink_matrix):
    family_tally = family_representation.shape[0]
    polymer_extent = family_representation.shape[1]
    intermediate_breadth = couple_lhs_weights.shape[1]
    residue_float_mask = amino_presence.astype(jnp.float32)
    retained_family_entries = family_keep_flags.astype(jnp.float32) * residue_float_mask[None, :]
    rescaled_family_rep = reduced_numeric_kind(normalise_features_step(family_representation.astype(jnp.float32), -1))
    family_lhs_mapped = reduced_numeric_kind(jnp.einsum('ohp,pd->ohd', rescaled_family_rep, growth_multiple(couple_lhs_weights)) * retained_family_entries[:, :, None])
    family_rhs_mapped = reduced_numeric_kind(jnp.einsum('ohp,pd->ohd', rescaled_family_rep, growth_multiple(couple_rhs_weights)) * retained_family_entries[:, :, None])
    portion_number = 8
    port_portion_group = family_lhs_mapped.reshape(family_tally, polymer_extent // portion_number, portion_number, intermediate_breadth).transpose(1, 0, 2, 3)
    live_blocks = retained_family_entries.reshape(family_tally, polymer_extent // portion_number, portion_number).transpose(1, 0, 2)
    out_weight = growth_multiple(pairwise_final_matrix)

    def outer_block(item):
        port_segments, lives = item
        averaged_tensor_contraction = jnp.einsum('lyj,lnx->ynjx', port_segments, family_rhs_mapped)
        counts = jnp.einsum('si,sj->ij', lives, retained_family_entries)
        mean = reduced_numeric_kind(averaged_tensor_contraction / jnp.maximum(counts, 1.0)[:, :, None, None])
        flat = mean.reshape(portion_number * polymer_extent, intermediate_breadth * intermediate_breadth)
        return jnp.dot(flat, out_weight).reshape(portion_number, polymer_extent, -1)
    update = lax.map(outer_block, (port_portion_group, live_blocks)).reshape(polymer_extent, polymer_extent, -1)
    first = contact_embedding + update
    pair_normed = reduced_numeric_kind(normalise_features_step(first, -1))
    pair_live = residue_float_mask[:, None] * residue_float_mask[None, :]
    left_raw = jnp.einsum('ijz,zc->cij', pair_normed, growth_multiple(edge_source_matrix))
    channels = left_raw.shape[0] // 2
    left_panel = reduced_numeric_kind(left_raw[:channels] * jax.nn.sigmoid(left_raw[channels:]) * pair_live[None])
    right_raw = jnp.einsum('ijz,zc->cij', pair_normed, growth_multiple(edge_target_matrix))
    right_panel = reduced_numeric_kind(right_raw[:channels] * jax.nn.sigmoid(right_raw[channels:]) * pair_live[None])
    product = reduced_numeric_kind(jnp.einsum('cik,cjk->cij', left_panel, right_panel))
    mixed = reduced_numeric_kind(normalise_features_step(product, 0))
    gate = jax.nn.sigmoid(jnp.einsum('ijz,zy->ijy', pair_normed, growth_multiple(edge_final_sigmoid_matrix)))
    second = first + gate * jnp.einsum('cij,cz->ijz', mixed, growth_multiple(edge_final_matrix))
    first_weight = growth_multiple(feedforward_expand_matrix)
    second_weight = growth_multiple(feedforward_shrink_matrix)

    def finish(row_indices):
        normed_rows = reduced_numeric_kind(normalise_features_step(row_indices, -1))
        hidden = reduced_numeric_kind(jax.nn.relu(jnp.dot(normed_rows, first_weight)))
        return row_indices + jnp.dot(hidden, second_weight)
    result = lax.map(finish, second.reshape(polymer_extent // portion_number, portion_number, polymer_extent, -1))
    return result.reshape(polymer_extent, polymer_extent, -1)
```

```python
import functools

import jax
import jax.numpy as jnp
from jax import lax
from jax.experimental import pallas as pl
from jax.experimental.pallas import tpu as pltpu
from jax.sharding import PartitionSpec as P

EPS = 1e-05
F32 = jnp.float32
BF16 = jnp.bfloat16
MESH = pl.DeviceIdType.MESH
VM = pl.BlockSpec(memory_space=pltpu.VMEM)
SM = pl.BlockSpec(memory_space=pltpu.SMEM)
ANY = pl.BlockSpec(memory_space=pl.ANY)
PACK = 4


def contract(a, b, da, db):
    return lax.dot_general(a, b, (((da,), (db,)), ((), ())), preferred_element_type=F32)


def normalise(v, axis):
    mean = jnp.mean(v, axis=axis, keepdims=True)
    cen = v - mean
    var = jnp.mean(cen * cen, axis=axis, keepdims=True)
    return cen * lax.rsqrt(var + EPS)


def project_kernel(fam, keep, amino, wl, wr, rsend, lsend, rsc):
    ns, tc, _ = fam.shape
    ch = wl.shape[1]
    x = lax.axis_index("cols")
    cols_live = amino[:, pl.ds(pl.multiple_of(x * tc, tc), tc)].astype(F32)
    live = keep[...].astype(F32) * cols_live
    live_t = live.T
    for g in range(ns // PACK):
        parts = []
        for k in range(PACK):
            s = g * PACK + k
            xn = normalise(fam[s], -1).astype(BF16)
            rt = contract(wr[...], xn, 0, 1) * live[s : s + 1, :]
            rsc[pl.ds(s, ch, stride=ns), :] = rt
            parts.append(
                jnp.dot(xn, wl[...], preferred_element_type=F32) * live_t[:, s : s + 1]
            )
        lsend[g] = jnp.concatenate(parts, axis=1).astype(BF16)
    rsend[0:ch] = rsc[...].reshape(ch, ns, tc).astype(BF16)
    rsend[ch] = live.astype(BF16)


def full_barrier(rows, cols, r, x):
    n = rows * cols
    me = r * cols + x
    barrier = pltpu.get_barrier_semaphore()

    def greet(t, carry):
        other = lax.rem(me + t, n)
        pl.semaphore_signal(
            barrier,
            inc=1,
            device_id={"rows": other // cols, "cols": lax.rem(other, cols)},
            device_id_type=MESH,
        )
        return carry

    lax.fori_loop(1, n, greet, 0)
    pl.semaphore_wait(barrier, n - 1)


def opm_exchange_kernel(
    rows, cols, tr, rsend, lsend, rbuf, lbuf, vbuf,
    rs_send, rs_recv, ls_send, ls_recv, vs_send, vs_recv, local
):
    r = lax.axis_index("rows")
    x = lax.axis_index("cols")
    ch = rsend.shape[0] - 1
    tc = lsend.shape[1]
    rpc = tc // tr
    outer = rows // 4
    o = r // 4
    m = lax.rem(r // 2, 2)
    k = lax.rem(r, 2)
    full_barrier(rows, cols, r, x)

    def row_of(oo, mm, kk):
        return (oo * 2 + mm) * 2 + kk

    def rcopy(block, dst_row, sem, first):
        return pltpu.make_async_remote_copy(
            src_ref=rsend if first else rbuf.at[block],
            dst_ref=rbuf.at[block],
            send_sem=rs_send.at[sem],
            recv_sem=rs_recv.at[block],
            device_id={"rows": dst_row},
            device_id_type=MESH,
        )

    def rwait(block):
        pltpu.make_async_copy(rsend, rbuf.at[block], rs_recv.at[block]).wait()

    mate = row_of(o, m, 1 - k)
    side = row_of(o, 1 - m, k)
    sends = []
    for t in range(1, outer):
        sends.append(rcopy(r, row_of(lax.rem(o + t, outer), m, k), t - 1, True))
        sends[-1].start()
    sends.append(rcopy(r, side, outer - 1, True))
    sends[-1].start()
    sends.append(rcopy(r, mate, outer, True))
    sends[-1].start()
    own_r = pltpu.make_async_copy(rsend, rbuf.at[r], local.at[0])
    own_r.start()

    def lcopy(t, xx):
        return pltpu.make_async_remote_copy(
            src_ref=lsend.at[:, pl.ds(pl.multiple_of(t * tr, tr), tr), :],
            dst_ref=lbuf.at[r],
            send_sem=ls_send.at[t * cols + xx],
            recv_sem=ls_recv.at[r],
            device_id={"rows": x * rpc + t, "cols": xx},
            device_id_type=MESH,
        )

    def vcopy(t, xx):
        return pltpu.make_async_remote_copy(
            src_ref=rsend.at[ch],
            dst_ref=vbuf.at[r],
            send_sem=vs_send.at[t * cols + xx],
            recv_sem=vs_recv.at[r],
            device_id={"rows": x * rpc + t, "cols": xx},
            device_id_type=MESH,
        )

    mine = lax.rem(r, rpc)
    home = r // rpc

    def lsends(q, carry):
        t = q // cols
        xx = lax.rem(q, cols)

        @pl.when(jnp.logical_not(jnp.logical_and(x * rpc + t == r, xx == x)))
        def _():
            vcopy(t, xx).start()
            lcopy(t, xx).start()

        return carry

    lax.fori_loop(0, rpc * cols, lsends, 0)

    @pl.when(home == x)
    def _():
        a = pltpu.make_async_copy(
            lsend.at[:, pl.ds(pl.multiple_of(mine * tr, tr), tr), :], lbuf.at[r], local.at[1]
        )
        b = pltpu.make_async_copy(rsend.at[ch], vbuf.at[r], local.at[2])
        a.start()
        b.start()
        a.wait()
        b.wait()

    sem = outer + 1
    for t in range(1, outer):
        block = row_of(lax.rem(o + outer - t, outer), m, k)
        rwait(block)
        for dst in (side, mate):
            sends.append(rcopy(block, dst, sem, False))
            sends[-1].start()
            sem += 1
    for t in range(outer):
        block = row_of(lax.rem(o + outer - t, outer), 1 - m, k)
        rwait(block)
        sends.append(rcopy(block, mate, sem, False))
        sends[-1].start()
        sem += 1
    for t in range(outer):
        for mm in range(2):
            rwait(row_of(lax.rem(o + outer - t, outer), mm, 1 - k))
    own_r.wait()
    for s in sends:
        s.wait_send()

    def lwaits(q, carry):
        t = q // cols
        xx = lax.rem(q, cols)

        @pl.when(jnp.logical_not(jnp.logical_and(x * rpc + t == r, xx == x)))
        def _():
            vcopy(t, xx).wait_send()
            lcopy(t, xx).wait_send()

        return carry

    lax.fori_loop(0, rpc * cols, lwaits, 0)

    def lrecvs(src, carry):
        @pl.when(jnp.logical_not(jnp.logical_and(src == r, home == x)))
        def _():
            pltpu.make_async_copy(
                lsend.at[:, pl.ds(0, tr), :], lbuf.at[src], ls_recv.at[src]
            ).wait()
            pltpu.make_async_copy(rsend.at[ch], vbuf.at[src], vs_recv.at[src]).wait()

        return carry

    lax.fori_loop(0, rows, lrecvs, 0)


def outer_kernel(
    amino, amino_v, rbuf, lbuf, vbuf, contact, w2t, es, et, efs,
    lp, rp, first, gate, lf, lmat, cnts, acts, lsc, rsc
):
    rows, groups, tr, lanes = lbuf.shape
    ns = rbuf.shape[2]
    ch = rbuf.shape[1] - 1
    tc = rbuf.shape[3]
    total = rows * ns
    rg = rows * groups
    rpc = tc // tr
    zc = es.shape[1] // 2
    r = lax.axis_index("rows")
    x = lax.axis_index("cols")
    lf[...] = lbuf[...].astype(F32).reshape(rg * tr, lanes)
    place = (
        lax.broadcasted_iota(jnp.int32, (rg, total), 1) // PACK
        == lax.broadcasted_iota(jnp.int32, (rg, total), 0)
    ).astype(F32).astype(BF16)
    keep = lax.rem(
        lax.broadcasted_iota(jnp.int32, (lanes, total), 1), PACK
    ) == lax.broadcasted_iota(jnp.int32, (lanes, total), 0) // ch
    for i in range(tr):
        t = lf[pl.ds(i, rg, stride=tr), :].astype(BF16)
        y = jnp.where(keep, contract(t, place, 0, 0), 0.0)
        acc = y[0:ch]
        for q in range(1, PACK):
            acc = acc + y[q * ch : (q + 1) * ch]
        lmat[i * ch : (i + 1) * ch, :] = acc.astype(BF16)
    v_left = vbuf[...].astype(F32).reshape(total, tc).astype(BF16)
    v_right = rbuf[:, ch].astype(F32).reshape(total, tc).astype(BF16)
    cnts[...] = contract(v_left, v_right, 0, 0)
    own = lax.rem(r, rpc)
    inv = 1.0 / jnp.maximum(cnts[pl.ds(pl.multiple_of(own * tr, tr), tr), :], 1.0)

    def outer(d, carry):
        rd = rbuf[:, d].astype(F32).reshape(total, tc).astype(BF16)
        a = jnp.dot(lmat[...], rd, preferred_element_type=F32).reshape(tr, ch, tc)
        acts[:, pl.ds(pl.multiple_of(d * ch, ch), ch), :] = (a * inv[:, None, :]).astype(BF16)
        return carry

    lax.fori_loop(0, ch, outer, 0, unroll=4)
    cols_live = amino_v[:, pl.ds(pl.multiple_of(x * tc, tc), tc)].astype(F32)

    for i in range(tr):
        f = contact[i].T + jnp.dot(w2t[...], acts[i], preferred_element_type=F32)
        first[i] = f
        pn = normalise(f, 0).astype(BF16)
        mask = cols_live * amino[r * tr + i].astype(F32)
        raw = contract(es[...], pn, 0, 0)
        lsc[pl.ds(i, zc, stride=tr), :] = raw[:zc] * jax.nn.sigmoid(raw[zc:]) * mask
        raw = contract(et[...], pn, 0, 0)
        rsc[pl.ds(i, zc, stride=tr), :] = raw[:zc] * jax.nn.sigmoid(raw[zc:]) * mask
        gate[i] = jax.nn.sigmoid(contract(efs[...], pn, 0, 0))
    lp[...] = lsc[...].reshape(zc, tr, tc).astype(BF16)
    rp[...] = rsc[...].reshape(zc, tr, tc).astype(BF16)


def triangle_kernel(
    rows, cols, lp, rp, pbuf, lfull, rfull, prod,
    l_send, l_recv, r_send, r_recv, p_send, p_recv, local
):
    r = lax.axis_index("rows")
    x = lax.axis_index("cols")
    n = rows * cols
    me = r * cols + x
    own = lfull.shape[0]
    tr, tc = lp.shape[1:]
    full_barrier(rows, cols, r, x)

    def tile(ref, rr, xx):
        return ref.at[
            :, pl.ds(pl.multiple_of(rr * tr, tr), tr), pl.ds(pl.multiple_of(xx * tc, tc), tc)
        ]

    def panel(src, dst, t, send, recv):
        other = lax.rem(me + t, n)
        return pltpu.make_async_remote_copy(
            src_ref=src.at[pl.ds(other * own, own)],
            dst_ref=tile(dst, r, x),
            send_sem=send.at[t],
            recv_sem=recv.at[t],
            device_id={"rows": other // cols, "cols": lax.rem(other, cols)},
            device_id_type=MESH,
        )

    def back(t):
        other = lax.rem(me + t, n)
        rr = other // cols
        xx = lax.rem(other, cols)
        return pltpu.make_async_remote_copy(
            src_ref=tile(prod, rr, xx),
            dst_ref=pbuf.at[pl.ds(me * own, own)],
            send_sem=p_send.at[t],
            recv_sem=p_recv.at[t],
            device_id={"rows": rr, "cols": xx},
            device_id_type=MESH,
        )

    def start(t, carry):
        panel(lp, lfull, t, l_send, l_recv).start()
        panel(rp, rfull, t, r_send, r_recv).start()
        return carry

    lax.fori_loop(1, n, start, 0)
    a = pltpu.make_async_copy(lp.at[pl.ds(me * own, own)], tile(lfull, r, x), local.at[0])
    b = pltpu.make_async_copy(rp.at[pl.ds(me * own, own)], tile(rfull, r, x), local.at[1])
    a.start()
    b.start()
    a.wait()
    b.wait()

    def finish(t, carry):
        src = lax.rem(me + n - t, n)
        rr = src // cols
        xx = lax.rem(src, cols)
        pltpu.make_async_copy(lp.at[pl.ds(0, own)], tile(lfull, rr, xx), l_recv.at[t]).wait()
        pltpu.make_async_copy(rp.at[pl.ds(0, own)], tile(rfull, rr, xx), r_recv.at[t]).wait()
        return carry

    lax.fori_loop(1, n, finish, 0)
    for c in range(own):
        prod[c] = contract(lfull[c], rfull[c], 1, 1).astype(BF16)

    def send_back(t, carry):
        back(t).start()
        return carry

    lax.fori_loop(1, n, send_back, 0)
    a = pltpu.make_async_copy(tile(prod, r, x), pbuf.at[pl.ds(me * own, own)], local.at[0])
    a.start()
    a.wait()

    def drain(t, carry):
        src = lax.rem(me + n - t, n)
        pltpu.make_async_copy(
            lp.at[pl.ds(0, own)], pbuf.at[pl.ds(src * own, own)], p_recv.at[t]
        ).wait()
        panel(lp, lfull, t, l_send, l_recv).wait_send()
        panel(rp, rfull, t, r_send, r_recv).wait_send()
        back(t).wait_send()
        return carry

    lax.fori_loop(1, n, drain, 0)


def final_kernel(pbuf, first, gate, ef, fe, fs, out, sc):
    zc, tr, tc = pbuf.shape
    sc[...] = normalise(pbuf[...].astype(F32), 0).reshape(zc * tr, tc)
    for i in range(tr):
        mixed = sc[pl.ds(i, zc, stride=tr), :].astype(BF16)
        second = first[i] + gate[i] * contract(ef[...], mixed, 0, 0)
        tn = normalise(second, 0).astype(BF16)
        hidden = jax.nn.relu(contract(fe[...], tn, 0, 0)).astype(BF16)
        out[i] = (second + contract(fs[...], hidden, 0, 0)).T


def params(**kw):
    return pltpu.CompilerParams(vmem_limit_bytes=60 * 1024 * 1024, **kw)


def on_device(fam, keep, amino, contact, wl, wr, pf, es, et, efs, ef, fe, fs):
    rows = lax.axis_size("rows")
    cols = lax.axis_size("cols")
    ns, tc, _ = fam.shape
    tr = contact.shape[0]
    ch = wl.shape[1]
    z = contact.shape[2]
    zc = es.shape[1] // 2
    groups = ns // PACK
    lanes = PACK * ch
    n = rows * cols
    own = zc // n
    rpc = tc // tr
    total = rows * ns
    dma = pltpu.SemaphoreType.DMA
    amino_v = amino.reshape(1, -1)
    w2t = pf.reshape(ch, ch, z).transpose(2, 1, 0).reshape(z, ch * ch)
    sds = jax.ShapeDtypeStruct
    rsend, lsend = pl.pallas_call(
        project_kernel,
        out_shape=(sds((ch + 1, ns, tc), BF16), sds((groups, tc, lanes), BF16)),
        in_specs=[VM] * 5,
        out_specs=(VM, VM),
        scratch_shapes=[pltpu.VMEM((ch * ns, tc), F32)],
        compiler_params=params(),
        name="project",
    )(fam, keep, amino_v, wl, wr)
    nsem = (rows // 4) + 1 + 2 * (rows // 4 - 1) + rows // 4
    rbuf, lbuf, vbuf = pl.pallas_call(
        functools.partial(opm_exchange_kernel, rows, cols, tr),
        out_shape=(
            sds((rows, ch + 1, ns, tc), BF16),
            sds((rows, groups, tr, lanes), BF16),
            sds((rows, ns, tc), BF16),
        ),
        in_specs=[VM, VM],
        out_specs=(VM, VM, VM),
        scratch_shapes=[
            dma((nsem,)), dma((rows,)), dma((rpc * cols,)), dma((rows,)),
            dma((rpc * cols,)), dma((rows,)), dma((3,)),
        ],
        compiler_params=params(collective_id=0, has_side_effects=True),
        name="opm_exchange",
    )(rsend, lsend)
    lp, rp, first, gate = pl.pallas_call(
        outer_kernel,
        out_shape=(
            sds((zc, tr, tc), BF16), sds((zc, tr, tc), BF16),
            sds((tr, z, tc), F32), sds((tr, z, tc), F32),
        ),
        in_specs=[SM] + [VM] * 9,
        out_specs=(VM,) * 4,
        scratch_shapes=[
            pltpu.VMEM((rows * groups * tr, lanes), F32),
            pltpu.VMEM((tr * ch, total), BF16),
            pltpu.VMEM((tc, tc), F32),
            pltpu.VMEM((tr, ch * ch, tc), BF16),
            pltpu.VMEM((zc * tr, tc), F32),
            pltpu.VMEM((zc * tr, tc), F32),
        ],
        compiler_params=params(),
        name="outer",
    )(amino, amino_v, rbuf, lbuf, vbuf, contact, w2t, es, et, efs)
    pbuf = pl.pallas_call(
        functools.partial(triangle_kernel, rows, cols),
        out_shape=sds((zc, tr, tc), BF16),
        in_specs=[VM, VM],
        out_specs=VM,
        scratch_shapes=[
            pltpu.VMEM((own, rows * tr, cols * tc), BF16),
            pltpu.VMEM((own, rows * tr, cols * tc), BF16),
            pltpu.VMEM((own, rows * tr, cols * tc), BF16),
        ] + [dma((n,))] * 6 + [dma((2,))],
        compiler_params=params(collective_id=1, has_side_effects=True),
        name="triangle",
    )(lp, rp)
    return pl.pallas_call(
        final_kernel,
        out_shape=sds((tr, tc, z), F32),
        in_specs=[VM] * 6,
        out_specs=VM,
        scratch_shapes=[pltpu.VMEM((zc * tr, tc), F32)],
        compiler_params=params(),
        name="final",
    )(pbuf, first, gate, ef, fe, fs)


def solution(mesh):
    tile3 = P(("crops", "rows"), "cols", None)
    in_specs = (tile3, P(("crops", "rows"), "cols"), P("crops"), tile3) + (P(),) * 9
    return jax.shard_map(
        on_device, mesh=mesh, in_specs=in_specs, out_specs=tile3, check_vma=False
    )
```

```python
import functools

import jax
import jax.numpy as jnp
from jax import lax
from jax.experimental import pallas as pl
from jax.experimental.pallas import tpu as pltpu
from jax.sharding import PartitionSpec as P

EPS = 1e-05
F32 = jnp.float32
BF16 = jnp.bfloat16
MESH = pl.DeviceIdType.MESH
VM = pl.BlockSpec(memory_space=pltpu.VMEM)
SM = pl.BlockSpec(memory_space=pltpu.SMEM)
ANY = pl.BlockSpec(memory_space=pl.ANY)
PACK = 4


def contract(a, b, da, db):
    return lax.dot_general(a, b, (((da,), (db,)), ((), ())), preferred_element_type=F32)


def normalise(v, axis):
    mean = jnp.mean(v, axis=axis, keepdims=True)
    cen = v - mean
    var = jnp.mean(cen * cen, axis=axis, keepdims=True)
    return cen * lax.rsqrt(var + EPS)


def fused_kernel(
    rows, cols, dims,
    fam, keep, amino, amino_v, contact_any, wl, wr, w2t_any, es, et, efs, ef, fe, fs,
    out,
    rsend, lsend, prs, rbuf, lbuf, vbuf, contact, w2t,
    lf, lmat, cnts, acts, psc, lp, rp, first, gate, pns,
    lfull, rfull, prod, pbuf,
    rs_send, rs_recv, ls_send, ls_recv, lx_send, vx_send, vs_recv,
    pl_send, pl_recv, pr_send, pr_recv, pb_send, pb_recv, local,
):
    ns, tc, tr, ch, wide = dims
    x = lax.axis_index("cols")
    r = lax.axis_index("rows")
    n = rows * cols
    me = r * cols + x
    rpc = tc // tr
    outer = rows // 4
    groups = ns // PACK
    lanes = PACK * ch
    total = rows * ns
    rg = rows * groups
    own = lfull.shape[0]
    zc = es.shape[1] // 2
    mine = lax.rem(r, rpc)
    home = r // rpc
    barrier = pltpu.get_barrier_semaphore()

    def peer(t):
        other = lax.rem(me + t, n)
        return other, other // cols, lax.rem(other, cols)

    def greet(t, carry):
        _, rr, xx = peer(t)
        pl.semaphore_signal(
            barrier, inc=1, device_id={"rows": rr, "cols": xx}, device_id_type=MESH
        )
        return carry

    lax.fori_loop(1, n, greet, 0)
    load_contact = pltpu.make_async_copy(contact_any, contact, local.at[3])
    load_w2t = pltpu.make_async_copy(w2t_any, w2t, local.at[4])
    load_contact.start()
    load_w2t.start()

    cols_live = amino_v[:, pl.ds(pl.multiple_of(x * tc, tc), tc)].astype(F32)
    live = keep[...].astype(F32) * cols_live
    live_t = live.T
    for g in range(groups):
        parts = []
        for k in range(PACK):
            s = g * PACK + k
            xn = normalise(fam[s], -1).astype(BF16)
            prs[pl.ds(s, ch, stride=ns), :] = contract(wr[...], xn, 1, 1) * live[s : s + 1, :]
            parts.append(contract(xn, wl[...], 1, 1) * live_t[:, s : s + 1])
        lsend[g] = jnp.concatenate(parts, axis=1).astype(BF16)
    rsend[0:ch] = prs[...].reshape(ch, ns, tc).astype(BF16)
    rsend[ch] = live.astype(BF16)
    pl.semaphore_wait(barrier, n - 1)

    o = r // 4
    m = lax.rem(r // 2, 2)
    k = lax.rem(r, 2)

    def row_of(oo, mm, kk):
        return (oo * 2 + mm) * 2 + kk

    def rcopy(block, dst_row, sem, fresh):
        return pltpu.make_async_remote_copy(
            src_ref=rsend if fresh else rbuf.at[block],
            dst_ref=rbuf.at[block],
            send_sem=rs_send.at[sem],
            recv_sem=rs_recv.at[block],
            device_id={"rows": dst_row},
            device_id_type=MESH,
        )

    def rwait(block):
        pltpu.make_async_copy(rsend, rbuf.at[block], rs_recv.at[block]).wait()

    mate = row_of(o, m, 1 - k)
    side = row_of(o, 1 - m, k)
    sends = []
    for t in range(1, outer):
        sends.append(rcopy(r, row_of(lax.rem(o + t, outer), m, k), t - 1, True))
        sends[-1].start()
    sends.append(rcopy(r, side, outer - 1, True))
    sends[-1].start()
    sends.append(rcopy(r, mate, outer, True))
    sends[-1].start()
    own_r = pltpu.make_async_copy(rsend, rbuf.at[r], local.at[0])
    own_r.start()

    def lcopy(t):
        return pltpu.make_async_remote_copy(
            src_ref=lsend.at[:, pl.ds(pl.multiple_of(t * tr, tr), tr), :],
            dst_ref=lbuf.at[r],
            send_sem=ls_send.at[t],
            recv_sem=ls_recv.at[r],
            device_id={"rows": x * rpc + t},
            device_id_type=MESH,
        )

    def lsends(t, carry):
        @pl.when(x * rpc + t != r)
        def _():
            lcopy(t).start()

        return carry

    lax.fori_loop(0, rpc, lsends, 0)

    @pl.when(home == x)
    def _():
        a = pltpu.make_async_copy(
            lsend.at[:, pl.ds(pl.multiple_of(mine * tr, tr), tr), :], lbuf.at[r], local.at[1]
        )
        a.start()
        a.wait()

    def lwait(block):
        pltpu.make_async_copy(
            lsend.at[:, pl.ds(0, tr), :], lbuf.at[block], ls_recv.at[block]
        ).wait()

    def hand(block, step, left):
        return pltpu.make_async_remote_copy(
            src_ref=lbuf.at[block] if left else rbuf.at[block, ch],
            dst_ref=lbuf.at[block] if left else vbuf.at[block],
            send_sem=(lx_send if left else vx_send).at[block, step - 1],
            recv_sem=(ls_recv if left else vs_recv).at[block],
            device_id={"cols": lax.rem(x + step, cols)},
            device_id_type=MESH,
        )

    sem = outer + 1
    for t in range(1, outer):
        block = row_of(lax.rem(o + outer - t, outer), m, k)
        rwait(block)
        for dst in (side, mate):
            sends.append(rcopy(block, dst, sem, False))
            sends[-1].start()
            sem += 1

    @pl.when(home == x)
    def _():
        def forward(t, carry):
            block = lax.rem(r + t, rows)

            @pl.when(block != r)
            def _():
                lwait(block)

            for step in range(1, cols):
                hand(block, step, True).start()
            return carry

        lax.fori_loop(0, rows, forward, 0)

    for t in range(outer):
        block = row_of(lax.rem(o + outer - t, outer), 1 - m, k)
        rwait(block)
        sends.append(rcopy(block, mate, sem, False))
        sends[-1].start()
        sem += 1
    own_r.wait()
    for t in range(outer):
        for mm in range(2):
            rwait(row_of(lax.rem(o + outer - t, outer), mm, 1 - k))

    @pl.when(home == x)
    def _():
        def forward(block, carry):
            for step in range(1, cols):
                hand(block, step, False).start()
            return carry

        lax.fori_loop(0, rows, forward, 0)
        vbuf[...] = rbuf[:, ch]

    @pl.when(home != x)
    def _():
        def take(block, carry):
            lwait(block)
            return carry

        lax.fori_loop(0, rows, take, 0)

    lf[...] = lbuf[...].astype(F32).reshape(rg * tr, lanes)
    place = (
        lax.broadcasted_iota(jnp.int32, (rg, total), 1) // PACK
        == lax.broadcasted_iota(jnp.int32, (rg, total), 0)
    ).astype(F32).astype(BF16)
    pick = lax.rem(
        lax.broadcasted_iota(jnp.int32, (lanes, total), 1), PACK
    ) == lax.broadcasted_iota(jnp.int32, (lanes, total), 0) // ch
    for i in range(tr):
        y = contract(lf[pl.ds(i, rg, stride=tr), :].astype(BF16), place, 0, 0)
        y = jnp.where(pick, y, 0.0)
        acc = y[0:ch]
        for q in range(1, PACK):
            acc = acc + y[q * ch : (q + 1) * ch]
        lmat[i * ch : (i + 1) * ch, :] = acc.astype(BF16)

    @pl.when(home != x)
    def _():
        def take(block, carry):
            pltpu.make_async_copy(rsend.at[ch], vbuf.at[block], vs_recv.at[block]).wait()
            return carry

        lax.fori_loop(0, rows, take, 0)

    v_left = vbuf[...].astype(F32).reshape(total, tc).astype(BF16)
    v_right = rbuf[:, ch].astype(F32).reshape(total, tc).astype(BF16)
    cnts[...] = contract(v_left, v_right, 0, 0)
    inv = 1.0 / jnp.maximum(cnts[pl.ds(pl.multiple_of(mine * tr, tr), tr), :], 1.0)

    def outer_step(d, carry):
        rd = rbuf[:, d].astype(F32).reshape(total, tc).astype(BF16)
        a = jnp.dot(lmat[...], rd, preferred_element_type=F32).reshape(tr, ch, tc)
        acts[:, pl.ds(pl.multiple_of(d * ch, ch), ch), :] = (a * inv[:, None, :]).astype(BF16)
        return carry

    lax.fori_loop(0, ch, outer_step, 0, unroll=4)
    load_contact.wait()
    load_w2t.wait()

    def mask_of(g):
        return jnp.concatenate(
            [cols_live * amino[r * tr + g * wide + i].astype(F32) for i in range(wide)], axis=1
        )

    def panel_of(weight, pn, g):
        raw = contract(weight[...], pn, 0, 0)
        val = raw[:zc] * jax.nn.sigmoid(raw[zc:]) * mask_of(g)
        for i in range(wide):
            psc[pl.ds(g * wide + i, zc, stride=tr), :] = val[:, i * tc : (i + 1) * tc]

    for g in range(tr // wide):
        base = g * wide
        u = jnp.dot(
            w2t[...],
            jnp.concatenate([acts[base + i] for i in range(wide)], axis=1),
            preferred_element_type=F32,
        )
        f = jnp.concatenate([contact[base + i].T for i in range(wide)], axis=1) + u
        first[g] = f
        pn = normalise(f, 0).astype(BF16)
        pns[g] = pn
        panel_of(es, pn, g)
    lp[...] = psc[...].reshape(zc, tr, tc).astype(BF16)

    def tile(ref, rr, xx):
        return ref.at[
            pl.ds(pl.multiple_of(rr * tr, tr), tr), pl.ds(pl.multiple_of(xx * tc, tc), tc)
        ]

    def left_copy(t):
        other, rr, xx = peer(t)
        return pltpu.make_async_remote_copy(
            src_ref=lp.at[pl.ds(other * own, own)],
            dst_ref=lfull.at[
                :, pl.ds(pl.multiple_of(r * tr, tr), tr), pl.ds(pl.multiple_of(x * tc, tc), tc)
            ],
            send_sem=pl_send.at[t],
            recv_sem=pl_recv.at[t],
            device_id={"rows": rr, "cols": xx},
            device_id_type=MESH,
        )

    def right_copy(c, t):
        other, rr, xx = peer(t)
        return pltpu.make_async_remote_copy(
            src_ref=rp.at[other * own + c],
            dst_ref=tile(rfull.at[c], r, x),
            send_sem=pr_send.at[c, t],
            recv_sem=pr_recv.at[c, t],
            device_id={"rows": rr, "cols": xx},
            device_id_type=MESH,
        )

    def back_copy(c, t):
        _, rr, xx = peer(t)
        return pltpu.make_async_remote_copy(
            src_ref=tile(prod.at[c], rr, xx),
            dst_ref=pbuf.at[me * own + c],
            send_sem=pb_send.at[c, t],
            recv_sem=pb_recv.at[c, t],
            device_id={"rows": rr, "cols": xx},
            device_id_type=MESH,
        )

    def each(fn):
        def step(t, carry):
            fn(t)
            return carry

        lax.fori_loop(1, n, step, 0)

    each(lambda t: left_copy(t).start())
    own_l = pltpu.make_async_copy(
        lp.at[pl.ds(me * own, own)],
        lfull.at[:, pl.ds(pl.multiple_of(r * tr, tr), tr), pl.ds(pl.multiple_of(x * tc, tc), tc)],
        local.at[0],
    )
    own_l.start()
    for g in range(tr // wide):
        panel_of(et, pns[g], g)
    rp[...] = psc[...].reshape(zc, tr, tc).astype(BF16)
    for c in range(min(2, own)):
        each(lambda t: right_copy(c, t).start())
    own_p = []
    for c in range(own):
        own_p.append(
            pltpu.make_async_copy(rp.at[me * own + c], tile(rfull.at[c], r, x), local.at[5 + c])
        )
        own_p[-1].start()
    for g in range(tr // wide):
        gate[g] = jax.nn.sigmoid(contract(efs[...], pns[g], 0, 0))
    own_l.wait()

    def left_wait(t):
        _, rr, xx = peer(n - t)
        pltpu.make_async_copy(
            lp.at[pl.ds(0, own)],
            lfull.at[
                :, pl.ds(pl.multiple_of(rr * tr, tr), tr), pl.ds(pl.multiple_of(xx * tc, tc), tc)
            ],
            pl_recv.at[t],
        ).wait()

    def right_wait(c, t):
        _, rr, xx = peer(n - t)
        pltpu.make_async_copy(rp.at[0], tile(rfull.at[c], rr, xx), pr_recv.at[c, t]).wait()

    def back_wait(c, t):
        src, _, _ = peer(n - t)
        pltpu.make_async_copy(rp.at[0], pbuf.at[src * own + c], pb_recv.at[c, t]).wait()

    each(left_wait)
    own_b = []
    for c in range(own):
        own_p[c].wait()
        each(lambda t: right_wait(c, t))
        prod[c] = contract(lfull[c], rfull[c], 1, 1).astype(BF16)
        if c + 2 < own:
            each(lambda t: right_copy(c + 2, t).start())
        each(lambda t: back_copy(c, t).start())
        own_b.append(
            pltpu.make_async_copy(
                tile(prod.at[c], r, x), pbuf.at[me * own + c], local.at[5 + own + c]
            )
        )
        own_b[-1].start()

    for s in sends:
        s.wait_send()

    def lsent(t, carry):
        @pl.when(x * rpc + t != r)
        def _():
            lcopy(t).wait_send()

        return carry

    lax.fori_loop(0, rpc, lsent, 0)

    @pl.when(home == x)
    def _():
        def sent(block, carry):
            for step in range(1, cols):
                hand(block, step, True).wait_send()
                hand(block, step, False).wait_send()
            return carry

        lax.fori_loop(0, rows, sent, 0)

    each(lambda t: left_copy(t).wait_send())
    for c in range(own):
        each(lambda t: right_copy(c, t).wait_send())
    for c in range(own):
        own_b[c].wait()
        each(lambda t: back_wait(c, t))

    psc[...] = normalise(pbuf[...].astype(F32), 0).reshape(zc * tr, tc)
    for g in range(tr // wide):
        mixed = jnp.concatenate(
            [psc[pl.ds(g * wide + i, zc, stride=tr), :].astype(BF16) for i in range(wide)], axis=1
        )
        second = first[g] + gate[g] * contract(ef[...], mixed, 0, 0)
        tn = normalise(second, 0).astype(BF16)
        hidden = jax.nn.relu(contract(fe[...], tn, 0, 0)).astype(BF16)
        res = second + contract(fs[...], hidden, 0, 0)
        for i in range(wide):
            out[g * wide + i] = res[:, i * tc : (i + 1) * tc].T
    for c in range(own):
        each(lambda t: back_copy(c, t).wait_send())


def on_device(fam, keep, amino, contact, wl, wr, pf, es, et, efs, ef, fe, fs):
    rows = lax.axis_size("rows")
    cols = lax.axis_size("cols")
    ns, tc, _ = fam.shape
    tr, _, z = contact.shape
    ch = wl.shape[1]
    zc = es.shape[1] // 2
    groups = ns // PACK
    lanes = PACK * ch
    n = rows * cols
    own = zc // n
    rpc = tc // tr
    total = rows * ns
    wide = 4
    outer = rows // 4
    dma = pltpu.SemaphoreType.DMA
    vmem = pltpu.VMEM
    w2t = pf.reshape(ch, ch, z).transpose(2, 1, 0).reshape(z, ch * ch)
    nsem = outer + 1 + 2 * (outer - 1) + outer
    full = (own, rows * tr, cols * tc)
    return pl.pallas_call(
        functools.partial(fused_kernel, rows, cols, (ns, tc, tr, ch, wide)),
        out_shape=jax.ShapeDtypeStruct((tr, tc, z), F32),
        in_specs=[VM, VM, SM, VM, ANY, VM, VM, ANY] + [VM] * 6,
        out_specs=VM,
        scratch_shapes=[
            vmem((ch + 1, ns, tc), BF16),
            vmem((groups, tc, lanes), BF16),
            vmem((ch * ns, tc), F32),
            vmem((rows, ch + 1, ns, tc), BF16),
            vmem((rows, groups, tr, lanes), BF16),
            vmem((rows, ns, tc), BF16),
            vmem((tr, tc, z), F32),
            vmem((z, ch * ch), BF16),
            vmem((rows * groups * tr, lanes), F32),
            vmem((tr * ch, total), BF16),
            vmem((tc, tc), F32),
            vmem((tr, ch * ch, tc), BF16),
            vmem((zc * tr, tc), F32),
            vmem((zc, tr, tc), BF16),
            vmem((zc, tr, tc), BF16),
            vmem((tr // wide, z, wide * tc), F32),
            vmem((tr // wide, z, wide * tc), F32),
            vmem((tr // wide, z, wide * tc), BF16),
            vmem(full, BF16),
            vmem(full, BF16),
            vmem(full, BF16),
            vmem((zc, tr, tc), BF16),
            dma((nsem,)),
            dma((rows,)),
            dma((rpc,)),
            dma((rows,)),
            dma((rows, cols - 1)),
            dma((rows, cols - 1)),
            dma((rows,)),
            dma((n,)),
            dma((n,)),
            dma((own, n)),
            dma((own, n)),
            dma((own, n)),
            dma((own, n)),
            dma((5 + 2 * own,)),
        ],
        compiler_params=pltpu.CompilerParams(
            vmem_limit_bytes=60 * 1024 * 1024, collective_id=0, has_side_effects=True
        ),
        name="pair_block",
    )(fam, keep, amino, amino.reshape(1, -1), contact, wl.T, wr.T, w2t, es, et, efs, ef, fe, fs)


def solution(mesh):
    tile3 = P(("crops", "rows"), "cols", None)
    in_specs = (tile3, P(("crops", "rows"), "cols"), P("crops"), tile3) + (P(),) * 9
    return jax.shard_map(
        on_device, mesh=mesh, in_specs=in_specs, out_specs=tile3, check_vma=False
    )
```

```python
import functools

import jax
import jax.numpy as jnp
from jax import lax
from jax.experimental import pallas as pl
from jax.experimental.pallas import tpu as pltpu
from jax.sharding import PartitionSpec as P

EPS = 1e-05
F32 = jnp.float32
BF16 = jnp.bfloat16
MESH = pl.DeviceIdType.MESH
VM = pl.BlockSpec(memory_space=pltpu.VMEM)
SM = pl.BlockSpec(memory_space=pltpu.SMEM)
ANY = pl.BlockSpec(memory_space=pl.ANY)
PACK = 4


def contract(a, b, da, db):
    return lax.dot_general(a, b, (((da,), (db,)), ((), ())), preferred_element_type=F32)


def normalise(v, axis):
    mean = jnp.mean(v, axis=axis, keepdims=True)
    cen = v - mean
    var = jnp.mean(cen * cen, axis=axis, keepdims=True)
    return cen * lax.rsqrt(var + EPS)


def fused_kernel(
    rows, cols, dims,
    fam, keep, amino, amino_v, contact_any, wl, wr, pf_any, es, et, efs, ef, fe, fs,
    out,
    rsend, lsend, prs, rbuf, lbuf, vbuf, contact, pf, pf_wide, w2t,
    lf, lmat, cnts, acts, psc, lp, rp, first, gate, pns,
    lfull, rfull, prod, pbuf,
    rs_send, rs_recv, ls_send, ls_recv, lx_send, vx_send, vs_recv,
    pl_send, pl_recv, pr_send, pr_recv, pb_send, pb_recv, local,
):
    ns, tc, tr, ch, wide = dims
    x = lax.axis_index("cols")
    r = lax.axis_index("rows")
    n = rows * cols
    me = r * cols + x
    rpc = tc // tr
    outer = rows // 4
    groups = ns // PACK
    lanes = PACK * ch
    total = rows * ns
    rg = rows * groups
    own = lfull.shape[0]
    zc = es.shape[1] // 2
    mine = lax.rem(r, rpc)
    home = r // rpc
    barrier = pltpu.get_barrier_semaphore()

    def peer(t):
        other = lax.rem(me + t, n)
        return other, other // cols, lax.rem(other, cols)

    def greet(t, carry):
        _, rr, xx = peer(t)
        pl.semaphore_signal(
            barrier, inc=1, device_id={"rows": rr, "cols": xx}, device_id_type=MESH
        )
        return carry

    lax.fori_loop(1, n, greet, 0)
    load_contact = pltpu.make_async_copy(contact_any, contact, local.at[3])
    load_pf = pltpu.make_async_copy(pf_any, pf, local.at[4])
    load_contact.start()
    load_pf.start()

    cols_live = amino_v[:, pl.ds(pl.multiple_of(x * tc, tc), tc)].astype(F32)
    live = keep[...].astype(F32) * cols_live
    live_t = live.T
    for g in range(groups):
        parts = []
        for k in range(PACK):
            s = g * PACK + k
            xn = normalise(fam[s], -1).astype(BF16)
            prs[pl.ds(s, ch, stride=ns), :] = contract(wr[...], xn, 1, 1) * live[s : s + 1, :]
            parts.append(contract(xn, wl[...], 1, 1) * live_t[:, s : s + 1])
        lsend[g] = jnp.concatenate(parts, axis=1).astype(BF16)
    rsend[0:ch] = prs[...].reshape(ch, ns, tc).astype(BF16)
    rsend[ch] = live.astype(BF16)
    pl.semaphore_wait(barrier, n - 1)

    o = r // 4
    m = lax.rem(r // 2, 2)
    k = lax.rem(r, 2)

    def row_of(oo, mm, kk):
        return (oo * 2 + mm) * 2 + kk

    def rcopy(block, dst_row, sem, fresh):
        return pltpu.make_async_remote_copy(
            src_ref=rsend if fresh else rbuf.at[block],
            dst_ref=rbuf.at[block],
            send_sem=rs_send.at[sem],
            recv_sem=rs_recv.at[block],
            device_id={"rows": dst_row},
            device_id_type=MESH,
        )

    def rwait(block):
        pltpu.make_async_copy(rsend, rbuf.at[block], rs_recv.at[block]).wait()

    mate = row_of(o, m, 1 - k)
    side = row_of(o, 1 - m, k)
    sends = []
    for t in range(1, outer):
        sends.append(rcopy(r, row_of(lax.rem(o + t, outer), m, k), t - 1, True))
        sends[-1].start()
    sends.append(rcopy(r, side, outer - 1, True))
    sends[-1].start()
    sends.append(rcopy(r, mate, outer, True))
    sends[-1].start()
    own_r = pltpu.make_async_copy(rsend, rbuf.at[r], local.at[0])
    own_r.start()

    def lcopy(t):
        return pltpu.make_async_remote_copy(
            src_ref=lsend.at[:, pl.ds(pl.multiple_of(t * tr, tr), tr), :],
            dst_ref=lbuf.at[r],
            send_sem=ls_send.at[t],
            recv_sem=ls_recv.at[r],
            device_id={"rows": x * rpc + t},
            device_id_type=MESH,
        )

    def lsends(t, carry):
        @pl.when(x * rpc + t != r)
        def _():
            lcopy(t).start()

        return carry

    lax.fori_loop(0, rpc, lsends, 0)

    @pl.when(home == x)
    def _():
        a = pltpu.make_async_copy(
            lsend.at[:, pl.ds(pl.multiple_of(mine * tr, tr), tr), :], lbuf.at[r], local.at[1]
        )
        a.start()
        a.wait()

    def vcopy(t, step):
        return pltpu.make_async_remote_copy(
            src_ref=rsend.at[ch],
            dst_ref=vbuf.at[r],
            send_sem=vx_send.at[t, step - 1],
            recv_sem=vs_recv.at[r],
            device_id={"rows": x * rpc + t, "cols": lax.rem(x + step, cols)},
            device_id_type=MESH,
        )

    def vsends(t, carry):
        for step in range(1, cols):
            vcopy(t, step).start()
        return carry

    lax.fori_loop(0, rpc, vsends, 0)

    load_pf.wait()
    pf_wide[...] = pf[...].astype(F32)
    for d in range(ch):
        w2t[d * ch : (d + 1) * ch, :] = pf_wide[pl.ds(d, ch, stride=ch), :].astype(BF16)

    def lwait(block):
        pltpu.make_async_copy(
            lsend.at[:, pl.ds(0, tr), :], lbuf.at[block], ls_recv.at[block]
        ).wait()

    def hand(block, step):
        return pltpu.make_async_remote_copy(
            src_ref=lbuf.at[block],
            dst_ref=lbuf.at[block],
            send_sem=lx_send.at[block, step - 1],
            recv_sem=ls_recv.at[block],
            device_id={"cols": lax.rem(x + step, cols)},
            device_id_type=MESH,
        )

    sem = outer + 1
    for t in range(1, outer):
        block = row_of(lax.rem(o + outer - t, outer), m, k)
        rwait(block)
        for dst in (side, mate):
            sends.append(rcopy(block, dst, sem, False))
            sends[-1].start()
            sem += 1

    @pl.when(home == x)
    def _():
        def forward(t, carry):
            block = lax.rem(r + t, rows)

            @pl.when(block != r)
            def _():
                lwait(block)

            for step in range(1, cols):
                hand(block, step).start()
            return carry

        lax.fori_loop(0, rows, forward, 0)

    for t in range(outer):
        block = row_of(lax.rem(o + outer - t, outer), 1 - m, k)
        rwait(block)
        sends.append(rcopy(block, mate, sem, False))
        sends[-1].start()
        sem += 1
    @pl.when(home != x)
    def _():
        def take(block, carry):
            lwait(block)
            return carry

        lax.fori_loop(0, rows, take, 0)

    lf[...] = lbuf[...].astype(F32).reshape(rg * tr, lanes)
    place = (
        lax.broadcasted_iota(jnp.int32, (rg, total), 1) // PACK
        == lax.broadcasted_iota(jnp.int32, (rg, total), 0)
    ).astype(F32).astype(BF16)
    pick = lax.rem(
        lax.broadcasted_iota(jnp.int32, (lanes, total), 1), PACK
    ) == lax.broadcasted_iota(jnp.int32, (lanes, total), 0) // ch
    for i in range(tr):
        y = contract(lf[pl.ds(i, rg, stride=tr), :].astype(BF16), place, 0, 0)
        y = jnp.where(pick, y, 0.0)
        acc = y[0:ch]
        for q in range(1, PACK):
            acc = acc + y[q * ch : (q + 1) * ch]
        lmat[i * ch : (i + 1) * ch, :] = acc.astype(BF16)

    @pl.when(home != x)
    def _():
        def take(block, carry):
            pltpu.make_async_copy(rsend.at[ch], vbuf.at[block], vs_recv.at[block]).wait()
            return carry

        lax.fori_loop(0, rows, take, 0)

    own_r.wait()
    for t in range(outer):
        for mm in range(2):
            rwait(row_of(lax.rem(o + outer - t, outer), mm, 1 - k))

    @pl.when(home == x)
    def _():
        vbuf[...] = rbuf[:, ch]

    v_left = vbuf[...].astype(F32).reshape(total, tc).astype(BF16)
    v_right = rbuf[:, ch].astype(F32).reshape(total, tc).astype(BF16)
    cnts[...] = contract(v_left, v_right, 0, 0)
    inv = 1.0 / jnp.maximum(cnts[pl.ds(pl.multiple_of(mine * tr, tr), tr), :], 1.0)

    def slab(d):
        return rbuf[:, d].astype(F32).reshape(total, tc).astype(BF16)

    def outer_step(h, carry):
        rd = jnp.concatenate([slab(2 * h), slab(2 * h + 1)], axis=1)
        a = jnp.dot(lmat[...], rd, preferred_element_type=F32)
        for q in range(2):
            part = a[:, q * tc : (q + 1) * tc].reshape(tr, ch, tc) * inv[:, None, :]
            at = pl.multiple_of((2 * h + q) * ch, ch)
            acts[:, pl.ds(at, ch), :] = part.astype(BF16)
        return carry

    lax.fori_loop(0, ch // 2, outer_step, 0, unroll=2)
    load_contact.wait()

    def mask_of(g):
        return jnp.concatenate(
            [cols_live * amino[r * tr + g * wide + i].astype(F32) for i in range(wide)], axis=1
        )

    def panel_of(weight, pn, g):
        raw = contract(weight[...], pn, 0, 0)
        val = raw[:zc] * jax.nn.sigmoid(raw[zc:]) * mask_of(g)
        for i in range(wide):
            psc[pl.ds(g * wide + i, zc, stride=tr), :] = val[:, i * tc : (i + 1) * tc]

    for g in range(tr // wide):
        base = g * wide
        u = contract(
            w2t[...], jnp.concatenate([acts[base + i] for i in range(wide)], axis=1), 0, 0
        )
        f = jnp.concatenate([contact[base + i].T for i in range(wide)], axis=1) + u
        first[g] = f
        pn = normalise(f, 0).astype(BF16)
        pns[g] = pn
        panel_of(es, pn, g)
    lp[...] = psc[...].reshape(zc, tr, tc).astype(BF16)

    def tile(ref, rr, xx):
        return ref.at[
            pl.ds(pl.multiple_of(rr * tr, tr), tr), pl.ds(pl.multiple_of(xx * tc, tc), tc)
        ]

    def left_copy(t):
        other, rr, xx = peer(t)
        return pltpu.make_async_remote_copy(
            src_ref=lp.at[pl.ds(other * own, own)],
            dst_ref=lfull.at[
                :, pl.ds(pl.multiple_of(r * tr, tr), tr), pl.ds(pl.multiple_of(x * tc, tc), tc)
            ],
            send_sem=pl_send.at[t],
            recv_sem=pl_recv.at[t],
            device_id={"rows": rr, "cols": xx},
            device_id_type=MESH,
        )

    def right_copy(c, t):
        other, rr, xx = peer(t)
        return pltpu.make_async_remote_copy(
            src_ref=rp.at[other * own + c],
            dst_ref=tile(rfull.at[c], r, x),
            send_sem=pr_send.at[c, t],
            recv_sem=pr_recv.at[c, t],
            device_id={"rows": rr, "cols": xx},
            device_id_type=MESH,
        )

    def back_copy(c, t):
        _, rr, xx = peer(t)
        return pltpu.make_async_remote_copy(
            src_ref=tile(prod.at[c], rr, xx),
            dst_ref=pbuf.at[me * own + c],
            send_sem=pb_send.at[c, t],
            recv_sem=pb_recv.at[c, t],
            device_id={"rows": rr, "cols": xx},
            device_id_type=MESH,
        )

    def each(fn):
        def step(t, carry):
            fn(t)
            return carry

        lax.fori_loop(1, n, step, 0)

    each(lambda t: left_copy(t).start())
    own_l = pltpu.make_async_copy(
        lp.at[pl.ds(me * own, own)],
        lfull.at[:, pl.ds(pl.multiple_of(r * tr, tr), tr), pl.ds(pl.multiple_of(x * tc, tc), tc)],
        local.at[0],
    )
    own_l.start()
    for g in range(tr // wide):
        panel_of(et, pns[g], g)
    rp[...] = psc[...].reshape(zc, tr, tc).astype(BF16)
    for c in range(min(2, own)):
        each(lambda t: right_copy(c, t).start())
    own_p = []
    for c in range(own):
        own_p.append(
            pltpu.make_async_copy(rp.at[me * own + c], tile(rfull.at[c], r, x), local.at[5 + c])
        )
        own_p[-1].start()
    for g in range(tr // wide):
        gate[g] = jax.nn.sigmoid(contract(efs[...], pns[g], 0, 0))
    own_l.wait()

    def left_wait(t):
        _, rr, xx = peer(n - t)
        pltpu.make_async_copy(
            lp.at[pl.ds(0, own)],
            lfull.at[
                :, pl.ds(pl.multiple_of(rr * tr, tr), tr), pl.ds(pl.multiple_of(xx * tc, tc), tc)
            ],
            pl_recv.at[t],
        ).wait()

    def right_wait(c, t):
        _, rr, xx = peer(n - t)
        pltpu.make_async_copy(rp.at[0], tile(rfull.at[c], rr, xx), pr_recv.at[c, t]).wait()

    def back_wait(c, t):
        src, _, _ = peer(n - t)
        pltpu.make_async_copy(rp.at[0], pbuf.at[src * own + c], pb_recv.at[c, t]).wait()

    each(left_wait)
    own_b = []
    for c in range(own):
        own_p[c].wait()
        each(lambda t: right_wait(c, t))
        prod[c] = contract(lfull[c], rfull[c], 1, 1).astype(BF16)
        if c + 2 < own:
            each(lambda t: right_copy(c + 2, t).start())
        each(lambda t: back_copy(c, t).start())
        own_b.append(
            pltpu.make_async_copy(
                tile(prod.at[c], r, x), pbuf.at[me * own + c], local.at[5 + own + c]
            )
        )
        own_b[-1].start()

    for s in sends:
        s.wait_send()

    def lsent(t, carry):
        @pl.when(x * rpc + t != r)
        def _():
            lcopy(t).wait_send()

        for step in range(1, cols):
            vcopy(t, step).wait_send()
        return carry

    lax.fori_loop(0, rpc, lsent, 0)

    @pl.when(home == x)
    def _():
        def sent(block, carry):
            for step in range(1, cols):
                hand(block, step).wait_send()
            return carry

        lax.fori_loop(0, rows, sent, 0)

    each(lambda t: left_copy(t).wait_send())
    for c in range(own):
        each(lambda t: right_copy(c, t).wait_send())
    for c in range(own):
        own_b[c].wait()
        each(lambda t: back_wait(c, t))

    psc[...] = normalise(pbuf[...].astype(F32), 0).reshape(zc * tr, tc)
    for g in range(tr // wide):
        mixed = jnp.concatenate(
            [psc[pl.ds(g * wide + i, zc, stride=tr), :].astype(BF16) for i in range(wide)], axis=1
        )
        second = first[g] + gate[g] * contract(ef[...], mixed, 0, 0)
        tn = normalise(second, 0).astype(BF16)
        hidden = jax.nn.relu(contract(fe[...], tn, 0, 0)).astype(BF16)
        res = second + contract(fs[...], hidden, 0, 0)
        for i in range(wide):
            out[g * wide + i] = res[:, i * tc : (i + 1) * tc].T
    for c in range(own):
        each(lambda t: back_copy(c, t).wait_send())


def on_device(fam, keep, amino, contact, wl, wr, pf, es, et, efs, ef, fe, fs):
    rows = lax.axis_size("rows")
    cols = lax.axis_size("cols")
    ns, tc, _ = fam.shape
    tr, _, z = contact.shape
    ch = wl.shape[1]
    zc = es.shape[1] // 2
    groups = ns // PACK
    lanes = PACK * ch
    n = rows * cols
    own = zc // n
    rpc = tc // tr
    total = rows * ns
    wide = 4
    outer = rows // 4
    dma = pltpu.SemaphoreType.DMA
    vmem = pltpu.VMEM
    nsem = outer + 1 + 2 * (outer - 1) + outer
    full = (own, rows * tr, cols * tc)
    return pl.pallas_call(
        functools.partial(fused_kernel, rows, cols, (ns, tc, tr, ch, wide)),
        out_shape=jax.ShapeDtypeStruct((tr, tc, z), F32),
        in_specs=[VM, VM, SM, VM, ANY, VM, VM, ANY] + [VM] * 6,
        out_specs=VM,
        scratch_shapes=[
            vmem((ch + 1, ns, tc), BF16),
            vmem((groups, tc, lanes), BF16),
            vmem((ch * ns, tc), F32),
            vmem((rows, ch + 1, ns, tc), BF16),
            vmem((rows, groups, tr, lanes), BF16),
            vmem((rows, ns, tc), BF16),
            vmem((tr, tc, z), F32),
            vmem((ch * ch, z), BF16),
            vmem((ch * ch, z), F32),
            vmem((ch * ch, z), BF16),
            vmem((rows * groups * tr, lanes), F32),
            vmem((tr * ch, total), BF16),
            vmem((tc, tc), F32),
            vmem((tr, ch * ch, tc), BF16),
            vmem((zc * tr, tc), F32),
            vmem((zc, tr, tc), BF16),
            vmem((zc, tr, tc), BF16),
            vmem((tr // wide, z, wide * tc), F32),
            vmem((tr // wide, z, wide * tc), F32),
            vmem((tr // wide, z, wide * tc), BF16),
            vmem(full, BF16),
            vmem(full, BF16),
            vmem(full, BF16),
            vmem((zc, tr, tc), BF16),
            dma((nsem,)),
            dma((rows,)),
            dma((rpc,)),
            dma((rows,)),
            dma((rows, cols - 1)),
            dma((rpc, cols - 1)),
            dma((rows,)),
            dma((n,)),
            dma((n,)),
            dma((own, n)),
            dma((own, n)),
            dma((own, n)),
            dma((own, n)),
            dma((5 + 2 * own,)),
        ],
        compiler_params=pltpu.CompilerParams(
            vmem_limit_bytes=60 * 1024 * 1024, collective_id=0, has_side_effects=True
        ),
        name="pair_block",
    )(fam, keep, amino, amino.reshape(1, -1), contact, wl.T, wr.T, pf, es, et, efs, ef, fe, fs)


def solution(mesh):
    tile3 = P(("crops", "rows"), "cols", None)
    in_specs = (tile3, P(("crops", "rows"), "cols"), P("crops"), tile3) + (P(),) * 9
    return jax.shard_map(
        on_device, mesh=mesh, in_specs=in_specs, out_specs=tile3, check_vma=False
    )
```

```python
import functools
import math

import jax
import jax.numpy as jnp
from jax import lax
from jax.experimental import pallas as pl
from jax.experimental.pallas import tpu as pltpu
from jax.sharding import PartitionSpec as P

EPS = 1e-05
F32 = jnp.float32
BF16 = jnp.bfloat16
MESH = pl.DeviceIdType.MESH
VM = pl.BlockSpec(memory_space=pltpu.VMEM)
SM = pl.BlockSpec(memory_space=pltpu.SMEM)
ANY = pl.BlockSpec(memory_space=pl.ANY)
PACK = 4


def contract(a, b, da, db):
    return lax.dot_general(a, b, (((da,), (db,)), ((), ())), preferred_element_type=F32)


def normalise(v, axis):
    mean = jnp.mean(v, axis=axis, keepdims=True)
    cen = v - mean
    var = jnp.mean(cen * cen, axis=axis, keepdims=True)
    return cen * lax.rsqrt(var + EPS)


def fused_kernel(
    rows, cols, dims,
    fam, keep, amino, amino_v, contact_any, wl, wr, pf_any, es, et, efs, ef, fe, fs,
    out,
    rsend, lsend, prs, rbuf, lbuf, vbuf, contact, pf, pf_wide, pf_dc, w2t,
    lf, lmat, cnts, acts, psc, lp, rp, first, gate, pns,
    lfull, rfull, prod, pbuf,
    rs_send, rs_recv, ls_send, ls_recv, lx_send, vx_send, vs_recv,
    pl_send, pl_recv, pr_send, pr_recv, pb_send, pb_recv, local,
):
    ns, tc, tr, ch, wide = dims
    x = lax.axis_index("cols")
    r = lax.axis_index("rows")
    n = rows * cols
    me = r * cols + x
    rpc = tc // tr
    outer = rows // 4
    groups = ns // PACK
    lanes = PACK * ch
    total = rows * ns
    rg = rows * groups
    own = lfull.shape[0]
    zc = es.shape[1] // 2
    mine = lax.rem(r, rpc)
    home = r // rpc
    stride = n // 4 + 1
    while math.gcd(stride, n) != 1:
        stride += 1
    barrier = pltpu.get_barrier_semaphore()

    def peer(t):
        other = lax.rem(me + t * stride, n)
        return other, other // cols, lax.rem(other, cols)

    def greet(t, carry):
        _, rr, xx = peer(t)
        pl.semaphore_signal(
            barrier, inc=1, device_id={"rows": rr, "cols": xx}, device_id_type=MESH
        )
        return carry

    lax.fori_loop(1, n, greet, 0)
    load_contact = pltpu.make_async_copy(contact_any, contact, local.at[3])
    load_pf = pltpu.make_async_copy(pf_any, pf, local.at[4])
    load_contact.start()
    load_pf.start()

    cols_live = amino_v[:, pl.ds(pl.multiple_of(x * tc, tc), tc)].astype(F32)
    live = keep[...].astype(F32) * cols_live
    live_t = live.T
    for g in range(groups):
        parts = []
        for k in range(PACK):
            s = g * PACK + k
            xn = normalise(fam[s], -1).astype(BF16)
            prs[pl.ds(s, ch, stride=ns), :] = contract(wr[...], xn, 1, 1) * live[s : s + 1, :]
            parts.append(contract(xn, wl[...], 1, 1) * live_t[:, s : s + 1])
        lsend[g] = jnp.concatenate(parts, axis=1).astype(BF16)
    rsend[0:ch] = prs[...].reshape(ch, ns, tc).astype(BF16)
    rsend[ch] = live.astype(BF16)
    pl.semaphore_wait(barrier, n - 1)

    o = r // 4
    m = lax.rem(r // 2, 2)
    k = lax.rem(r, 2)

    def row_of(oo, mm, kk):
        return (oo * 2 + mm) * 2 + kk

    def rcopy(block, dst_row, sem, fresh):
        return pltpu.make_async_remote_copy(
            src_ref=rsend if fresh else rbuf.at[block],
            dst_ref=rbuf.at[block],
            send_sem=rs_send.at[sem],
            recv_sem=rs_recv.at[block],
            device_id={"rows": dst_row},
            device_id_type=MESH,
        )

    def rwait(block):
        pltpu.make_async_copy(rsend, rbuf.at[block], rs_recv.at[block]).wait()

    mate = row_of(o, m, 1 - k)
    side = row_of(o, 1 - m, k)
    sends = []
    for t in range(1, outer):
        sends.append(rcopy(r, row_of(lax.rem(o + t, outer), m, k), t - 1, True))
        sends[-1].start()
    sends.append(rcopy(r, side, outer - 1, True))
    sends[-1].start()
    sends.append(rcopy(r, mate, outer, True))
    sends[-1].start()
    own_r = pltpu.make_async_copy(rsend, rbuf.at[r], local.at[0])
    own_r.start()

    def lcopy(t):
        return pltpu.make_async_remote_copy(
            src_ref=lsend.at[:, pl.ds(pl.multiple_of(t * tr, tr), tr), :],
            dst_ref=lbuf.at[r],
            send_sem=ls_send.at[t],
            recv_sem=ls_recv.at[r],
            device_id={"rows": x * rpc + t},
            device_id_type=MESH,
        )

    def lsends(t, carry):
        @pl.when(x * rpc + t != r)
        def _():
            lcopy(t).start()

        return carry

    lax.fori_loop(0, rpc, lsends, 0)

    @pl.when(home == x)
    def _():
        a = pltpu.make_async_copy(
            lsend.at[:, pl.ds(pl.multiple_of(mine * tr, tr), tr), :], lbuf.at[r], local.at[1]
        )
        a.start()
        a.wait()

    def vcopy(t, step):
        return pltpu.make_async_remote_copy(
            src_ref=rsend.at[ch],
            dst_ref=vbuf.at[r],
            send_sem=vx_send.at[t, step - 1],
            recv_sem=vs_recv.at[r],
            device_id={"rows": x * rpc + t, "cols": lax.rem(x + step, cols)},
            device_id_type=MESH,
        )

    def vsends(t, carry):
        for step in range(1, cols):
            vcopy(t, step).start()
        return carry

    lax.fori_loop(0, rpc, vsends, 0)

    load_pf.wait()
    pf_wide[...] = pf[...].astype(F32)
    for d in range(ch):
        pf_dc[d * ch : (d + 1) * ch, :] = pf_wide[pl.ds(d, ch, stride=ch), :]

    def lwait(block):
        pltpu.make_async_copy(
            lsend.at[:, pl.ds(0, tr), :], lbuf.at[block], ls_recv.at[block]
        ).wait()

    def hand(block, step):
        return pltpu.make_async_remote_copy(
            src_ref=lbuf.at[block],
            dst_ref=lbuf.at[block],
            send_sem=lx_send.at[block, step - 1],
            recv_sem=ls_recv.at[block],
            device_id={"cols": lax.rem(x + step, cols)},
            device_id_type=MESH,
        )

    sem = outer + 1
    for t in range(1, outer):
        block = row_of(lax.rem(o + outer - t, outer), m, k)
        rwait(block)
        for dst in (side, mate):
            sends.append(rcopy(block, dst, sem, False))
            sends[-1].start()
            sem += 1

    @pl.when(home == x)
    def _():
        def forward(t, carry):
            block = lax.rem(r + t, rows)

            @pl.when(block != r)
            def _():
                lwait(block)

            for step in range(1, cols):
                hand(block, step).start()
            return carry

        lax.fori_loop(0, rows, forward, 0)

    for t in range(outer):
        block = row_of(lax.rem(o + outer - t, outer), 1 - m, k)
        rwait(block)
        sends.append(rcopy(block, mate, sem, False))
        sends[-1].start()
        sem += 1
    @pl.when(home != x)
    def _():
        def take(block, carry):
            lwait(block)
            return carry

        lax.fori_loop(0, rows, take, 0)

    lf[...] = lbuf[...].astype(F32).reshape(rg * tr, lanes)
    place = (
        lax.broadcasted_iota(jnp.int32, (rg, total), 1) // PACK
        == lax.broadcasted_iota(jnp.int32, (rg, total), 0)
    ).astype(F32).astype(BF16)
    pick = lax.rem(
        lax.broadcasted_iota(jnp.int32, (lanes, total), 1), PACK
    ) == lax.broadcasted_iota(jnp.int32, (lanes, total), 0) // ch
    for i in range(tr):
        y = contract(lf[pl.ds(i, rg, stride=tr), :].astype(BF16), place, 0, 0)
        y = jnp.where(pick, y, 0.0)
        acc = y[0:ch]
        for q in range(1, PACK):
            acc = acc + y[q * ch : (q + 1) * ch]
        lmat[i * ch : (i + 1) * ch, :] = acc.astype(BF16)

    @pl.when(home != x)
    def _():
        def take(block, carry):
            pltpu.make_async_copy(rsend.at[ch], vbuf.at[block], vs_recv.at[block]).wait()
            return carry

        lax.fori_loop(0, rows, take, 0)

    for q in range(0, ch * ch, tc):
        w2t[:, q : q + tc] = pf_dc[q : q + tc, :].T.astype(BF16)
    own_r.wait()
    for t in range(outer):
        for mm in range(2):
            rwait(row_of(lax.rem(o + outer - t, outer), mm, 1 - k))

    @pl.when(home == x)
    def _():
        vbuf[...] = rbuf[:, ch]

    v_left = vbuf[...].astype(F32).reshape(total, tc).astype(BF16)
    v_right = rbuf[:, ch].astype(F32).reshape(total, tc).astype(BF16)
    cnts[...] = contract(v_left, v_right, 0, 0)
    inv = 1.0 / jnp.maximum(cnts[pl.ds(pl.multiple_of(mine * tr, tr), tr), :], 1.0)

    def slab(d):
        return rbuf[:, d].astype(F32).reshape(total, tc).astype(BF16)

    def outer_step(h, carry):
        rd = jnp.concatenate([slab(2 * h), slab(2 * h + 1)], axis=1)
        a = jnp.dot(lmat[...], rd, preferred_element_type=F32)
        for q in range(2):
            part = a[:, q * tc : (q + 1) * tc].reshape(tr, ch, tc) * inv[:, None, :]
            at = pl.multiple_of((2 * h + q) * ch, ch)
            acts[:, pl.ds(at, ch), :] = part.astype(BF16)
        return carry

    lax.fori_loop(0, ch // 2, outer_step, 0, unroll=2)
    load_contact.wait()

    def mask_of(g):
        return jnp.concatenate(
            [cols_live * amino[r * tr + g * wide + i].astype(F32) for i in range(wide)], axis=1
        )

    def panel_of(weight, pn, g):
        raw = contract(weight[...], pn, 0, 0)
        val = raw[:zc] * jax.nn.sigmoid(raw[zc:]) * mask_of(g)
        for i in range(wide):
            psc[pl.ds(g * wide + i, zc, stride=tr), :] = val[:, i * tc : (i + 1) * tc]

    for g in range(tr // wide):
        base = g * wide
        u = jnp.dot(
            w2t[...],
            jnp.concatenate([acts[base + i] for i in range(wide)], axis=1),
            preferred_element_type=F32,
        )
        f = jnp.concatenate([contact[base + i].T for i in range(wide)], axis=1) + u
        first[g] = f
        pn = normalise(f, 0).astype(BF16)
        pns[g] = pn
        panel_of(es, pn, g)
    lp[...] = psc[...].reshape(zc, tr, tc).astype(BF16)

    def tile(ref, rr, xx):
        return ref.at[
            pl.ds(pl.multiple_of(rr * tr, tr), tr), pl.ds(pl.multiple_of(xx * tc, tc), tc)
        ]

    def left_copy(t):
        other, rr, xx = peer(t)
        return pltpu.make_async_remote_copy(
            src_ref=lp.at[pl.ds(other * own, own)],
            dst_ref=lfull.at[
                :, pl.ds(pl.multiple_of(r * tr, tr), tr), pl.ds(pl.multiple_of(x * tc, tc), tc)
            ],
            send_sem=pl_send.at[t],
            recv_sem=pl_recv.at[t],
            device_id={"rows": rr, "cols": xx},
            device_id_type=MESH,
        )

    def right_copy(c, t):
        other, rr, xx = peer(t)
        return pltpu.make_async_remote_copy(
            src_ref=rp.at[other * own + c],
            dst_ref=tile(rfull.at[c], r, x),
            send_sem=pr_send.at[c, t],
            recv_sem=pr_recv.at[c, t],
            device_id={"rows": rr, "cols": xx},
            device_id_type=MESH,
        )

    def back_copy(c, t):
        _, rr, xx = peer(t)
        return pltpu.make_async_remote_copy(
            src_ref=tile(prod.at[c], rr, xx),
            dst_ref=pbuf.at[me * own + c],
            send_sem=pb_send.at[c, t],
            recv_sem=pb_recv.at[c, t],
            device_id={"rows": rr, "cols": xx},
            device_id_type=MESH,
        )

    def each(fn):
        def step(t, carry):
            fn(t)
            return carry

        lax.fori_loop(1, n, step, 0)

    each(lambda t: left_copy(t).start())
    own_l = pltpu.make_async_copy(
        lp.at[pl.ds(me * own, own)],
        lfull.at[:, pl.ds(pl.multiple_of(r * tr, tr), tr), pl.ds(pl.multiple_of(x * tc, tc), tc)],
        local.at[0],
    )
    own_l.start()
    for g in range(tr // wide):
        panel_of(et, pns[g], g)
    rp[...] = psc[...].reshape(zc, tr, tc).astype(BF16)
    for c in range(min(2, own)):
        each(lambda t: right_copy(c, t).start())
    own_p = []
    for c in range(own):
        own_p.append(
            pltpu.make_async_copy(rp.at[me * own + c], tile(rfull.at[c], r, x), local.at[5 + c])
        )
        own_p[-1].start()
    for g in range(tr // wide):
        gate[g] = jax.nn.sigmoid(contract(efs[...], pns[g], 0, 0))
    own_l.wait()

    def left_wait(t):
        _, rr, xx = peer(n - t)
        pltpu.make_async_copy(
            lp.at[pl.ds(0, own)],
            lfull.at[
                :, pl.ds(pl.multiple_of(rr * tr, tr), tr), pl.ds(pl.multiple_of(xx * tc, tc), tc)
            ],
            pl_recv.at[t],
        ).wait()

    def right_wait(c, t):
        _, rr, xx = peer(n - t)
        pltpu.make_async_copy(rp.at[0], tile(rfull.at[c], rr, xx), pr_recv.at[c, t]).wait()

    def back_wait(c, t):
        src, _, _ = peer(n - t)
        pltpu.make_async_copy(rp.at[0], pbuf.at[src * own + c], pb_recv.at[c, t]).wait()

    each(left_wait)
    own_b = []
    for c in range(own):
        own_p[c].wait()
        each(lambda t: right_wait(c, t))
        prod[c] = contract(lfull[c], rfull[c], 1, 1).astype(BF16)
        if c + 2 < own:
            each(lambda t: right_copy(c + 2, t).start())
        each(lambda t: back_copy(c, t).start())
        own_b.append(
            pltpu.make_async_copy(
                tile(prod.at[c], r, x), pbuf.at[me * own + c], local.at[5 + own + c]
            )
        )
        own_b[-1].start()

    for s in sends:
        s.wait_send()

    def lsent(t, carry):
        @pl.when(x * rpc + t != r)
        def _():
            lcopy(t).wait_send()

        for step in range(1, cols):
            vcopy(t, step).wait_send()
        return carry

    lax.fori_loop(0, rpc, lsent, 0)

    @pl.when(home == x)
    def _():
        def sent(block, carry):
            for step in range(1, cols):
                hand(block, step).wait_send()
            return carry

        lax.fori_loop(0, rows, sent, 0)

    each(lambda t: left_copy(t).wait_send())
    for c in range(own):
        each(lambda t: right_copy(c, t).wait_send())
    for c in range(own):
        own_b[c].wait()
        each(lambda t: back_wait(c, t))

    psc[...] = normalise(pbuf[...].astype(F32), 0).reshape(zc * tr, tc)
    for g in range(tr // wide):
        mixed = jnp.concatenate(
            [psc[pl.ds(g * wide + i, zc, stride=tr), :].astype(BF16) for i in range(wide)], axis=1
        )
        second = first[g] + gate[g] * contract(ef[...], mixed, 0, 0)
        tn = normalise(second, 0).astype(BF16)
        hidden = jax.nn.relu(contract(fe[...], tn, 0, 0)).astype(BF16)
        res = second + contract(fs[...], hidden, 0, 0)
        for i in range(wide):
            out[g * wide + i] = res[:, i * tc : (i + 1) * tc].T
    for c in range(own):
        each(lambda t: back_copy(c, t).wait_send())


def on_device(fam, keep, amino, contact, wl, wr, pf, es, et, efs, ef, fe, fs):
    rows = lax.axis_size("rows")
    cols = lax.axis_size("cols")
    ns, tc, _ = fam.shape
    tr, _, z = contact.shape
    ch = wl.shape[1]
    zc = es.shape[1] // 2
    groups = ns // PACK
    lanes = PACK * ch
    n = rows * cols
    own = zc // n
    rpc = tc // tr
    total = rows * ns
    wide = 4
    outer = rows // 4
    dma = pltpu.SemaphoreType.DMA
    vmem = pltpu.VMEM
    nsem = outer + 1 + 2 * (outer - 1) + outer
    full = (own, rows * tr, cols * tc)
    return pl.pallas_call(
        functools.partial(fused_kernel, rows, cols, (ns, tc, tr, ch, wide)),
        out_shape=jax.ShapeDtypeStruct((tr, tc, z), F32),
        in_specs=[VM, VM, SM, VM, ANY, VM, VM, ANY] + [VM] * 6,
        out_specs=VM,
        scratch_shapes=[
            vmem((ch + 1, ns, tc), BF16),
            vmem((groups, tc, lanes), BF16),
            vmem((ch * ns, tc), F32),
            vmem((rows, ch + 1, ns, tc), BF16),
            vmem((rows, groups, tr, lanes), BF16),
            vmem((rows, ns, tc), BF16),
            vmem((tr, tc, z), F32),
            vmem((ch * ch, z), BF16),
            vmem((ch * ch, z), F32),
            vmem((ch * ch, z), F32),
            vmem((z, ch * ch), BF16),
            vmem((rows * groups * tr, lanes), F32),
            vmem((tr * ch, total), BF16),
            vmem((tc, tc), F32),
            vmem((tr, ch * ch, tc), BF16),
            vmem((zc * tr, tc), F32),
            vmem((zc, tr, tc), BF16),
            vmem((zc, tr, tc), BF16),
            vmem((tr // wide, z, wide * tc), F32),
            vmem((tr // wide, z, wide * tc), F32),
            vmem((tr // wide, z, wide * tc), BF16),
            vmem(full, BF16),
            vmem(full, BF16),
            vmem(full, BF16),
            vmem((zc, tr, tc), BF16),
            dma((nsem,)),
            dma((rows,)),
            dma((rpc,)),
            dma((rows,)),
            dma((rows, cols - 1)),
            dma((rpc, cols - 1)),
            dma((rows,)),
            dma((n,)),
            dma((n,)),
            dma((own, n)),
            dma((own, n)),
            dma((own, n)),
            dma((own, n)),
            dma((5 + 2 * own,)),
        ],
        compiler_params=pltpu.CompilerParams(
            vmem_limit_bytes=60 * 1024 * 1024, collective_id=0, has_side_effects=True
        ),
        name="pair_block",
    )(fam, keep, amino, amino.reshape(1, -1), contact, wl.T, wr.T, pf, es, et, efs, ef, fe, fs)


def solution(mesh):
    tile3 = P(("crops", "rows"), "cols", None)
    in_specs = (tile3, P(("crops", "rows"), "cols"), P("crops"), tile3) + (P(),) * 9
    return jax.shard_map(
        on_device, mesh=mesh, in_specs=in_specs, out_specs=tile3, check_vma=False
    )
```

```python
import functools
import math

import jax
import jax.numpy as jnp
from jax import lax
from jax.experimental import pallas as pl
from jax.experimental.pallas import tpu as pltpu
from jax.sharding import PartitionSpec as P

EPS = 1e-05
F32 = jnp.float32
BF16 = jnp.bfloat16
MESH = pl.DeviceIdType.MESH
VM = pl.BlockSpec(memory_space=pltpu.VMEM)
SM = pl.BlockSpec(memory_space=pltpu.SMEM)
ANY = pl.BlockSpec(memory_space=pl.ANY)
PACK = 4


def contract(a, b, da, db):
    return lax.dot_general(a, b, (((da,), (db,)), ((), ())), preferred_element_type=F32)


def normalise(v, axis):
    mean = jnp.mean(v, axis=axis, keepdims=True)
    cen = v - mean
    var = jnp.mean(cen * cen, axis=axis, keepdims=True)
    return cen * lax.rsqrt(var + EPS)


def fused_kernel(
    rows, cols, dims,
    fam, keep, amino, amino_v, contact_any, wl, wr, pf_any, es, et, efs, ef, fe, fs,
    out,
    rsend, lsend, prs, rbuf, lbuf, vbuf, contact, pf, pf_wide, pf_dc, w2t,
    lf, lmat, cnts, acts, psc, lp, rp, first, gate, pns,
    lfull, rfull, prod, pbuf,
    rs_send, rs_recv, ls_send, ls_recv, lx_send, vx_send, vs_recv,
    pl_send, pl_recv, pr_send, pr_recv, pb_send, pb_recv, local,
):
    ns, tc, tr, ch, wide = dims
    x = lax.axis_index("cols")
    r = lax.axis_index("rows")
    n = rows * cols
    me = r * cols + x
    rpc = tc // tr
    outer = rows // 4
    groups = ns // PACK
    lanes = PACK * ch
    total = rows * ns
    rg = rows * groups
    own = lfull.shape[0]
    zc = es.shape[1] // 2
    mine = lax.rem(r, rpc)
    home = r // rpc
    stride = n // 4 + 1
    while math.gcd(stride, n) != 1:
        stride += 1
    barrier = pltpu.get_barrier_semaphore()

    def peer(t):
        other = lax.rem(me + t * stride, n)
        return other, other // cols, lax.rem(other, cols)

    def greet(t, carry):
        _, rr, xx = peer(t)
        pl.semaphore_signal(
            barrier, inc=1, device_id={"rows": rr, "cols": xx}, device_id_type=MESH
        )
        return carry

    lax.fori_loop(1, n, greet, 0)
    load_contact = pltpu.make_async_copy(contact_any, contact, local.at[3])
    load_pf = pltpu.make_async_copy(pf_any, pf, local.at[4])
    load_contact.start()
    load_pf.start()

    cols_live = amino_v[:, pl.ds(pl.multiple_of(x * tc, tc), tc)].astype(F32)
    live = keep[...].astype(F32) * cols_live
    live_t = live.T
    for g in range(groups):
        parts = []
        for k in range(PACK):
            s = g * PACK + k
            xn = normalise(fam[s], -1).astype(BF16)
            prs[pl.ds(s, ch, stride=ns), :] = contract(wr[...], xn, 1, 1) * live[s : s + 1, :]
            parts.append(contract(xn, wl[...], 1, 1) * live_t[:, s : s + 1])
        lsend[g] = jnp.concatenate(parts, axis=1).astype(BF16)
    rsend[0:ch] = prs[...].reshape(ch, ns, tc).astype(BF16)
    rsend[ch] = live.astype(BF16)
    pl.semaphore_wait(barrier, n - 1)

    o = r // 4
    m = lax.rem(r // 2, 2)
    k = lax.rem(r, 2)

    def row_of(oo, mm, kk):
        return (oo * 2 + mm) * 2 + kk

    def rcopy(block, dst_row, sem, fresh):
        return pltpu.make_async_remote_copy(
            src_ref=rsend if fresh else rbuf.at[block],
            dst_ref=rbuf.at[block],
            send_sem=rs_send.at[sem],
            recv_sem=rs_recv.at[block],
            device_id={"rows": dst_row},
            device_id_type=MESH,
        )

    def rwait(block):
        pltpu.make_async_copy(rsend, rbuf.at[block], rs_recv.at[block]).wait()

    mate = row_of(o, m, 1 - k)
    side = row_of(o, 1 - m, k)
    sends = []
    for t in range(1, outer):
        sends.append(rcopy(r, row_of(lax.rem(o + t, outer), m, k), t - 1, True))
        sends[-1].start()
    sends.append(rcopy(r, side, outer - 1, True))
    sends[-1].start()
    sends.append(rcopy(r, mate, outer, True))
    sends[-1].start()
    own_r = pltpu.make_async_copy(rsend, rbuf.at[r], local.at[0])
    own_r.start()

    def lcopy(t):
        return pltpu.make_async_remote_copy(
            src_ref=lsend.at[:, pl.ds(pl.multiple_of(t * tr, tr), tr), :],
            dst_ref=lbuf.at[r],
            send_sem=ls_send.at[t],
            recv_sem=ls_recv.at[r],
            device_id={"rows": x * rpc + t},
            device_id_type=MESH,
        )

    def lsends(t, carry):
        @pl.when(x * rpc + t != r)
        def _():
            lcopy(t).start()

        return carry

    lax.fori_loop(0, rpc, lsends, 0)

    @pl.when(home == x)
    def _():
        a = pltpu.make_async_copy(
            lsend.at[:, pl.ds(pl.multiple_of(mine * tr, tr), tr), :], lbuf.at[r], local.at[1]
        )
        a.start()
        a.wait()

    def vcopy(t, step):
        return pltpu.make_async_remote_copy(
            src_ref=rsend.at[ch],
            dst_ref=vbuf.at[r],
            send_sem=vx_send.at[t, step - 1],
            recv_sem=vs_recv.at[r],
            device_id={"rows": x * rpc + t, "cols": lax.rem(x + step, cols)},
            device_id_type=MESH,
        )

    def vsends(t, carry):
        for step in range(1, cols):
            vcopy(t, step).start()
        return carry

    lax.fori_loop(0, rpc, vsends, 0)

    load_pf.wait()
    pf_wide[...] = pf[...].astype(F32)
    for d in range(ch):
        pf_dc[d * ch : (d + 1) * ch, :] = pf_wide[pl.ds(d, ch, stride=ch), :]

    def lwait(block):
        pltpu.make_async_copy(
            lsend.at[:, pl.ds(0, tr), :], lbuf.at[block], ls_recv.at[block]
        ).wait()

    def hand(block, step):
        return pltpu.make_async_remote_copy(
            src_ref=lbuf.at[block],
            dst_ref=lbuf.at[block],
            send_sem=lx_send.at[block, step - 1],
            recv_sem=ls_recv.at[block],
            device_id={"cols": lax.rem(x + step, cols)},
            device_id_type=MESH,
        )

    sem = outer + 1
    for t in range(1, outer):
        block = row_of(lax.rem(o + outer - t, outer), m, k)
        rwait(block)
        for dst in (side, mate):
            sends.append(rcopy(block, dst, sem, False))
            sends[-1].start()
            sem += 1

    @pl.when(home == x)
    def _():
        def forward(t, carry):
            block = lax.rem(r + t, rows)

            @pl.when(block != r)
            def _():
                lwait(block)

            for step in range(1, cols):
                hand(block, step).start()
            return carry

        lax.fori_loop(0, rows, forward, 0)

    for t in range(outer):
        block = row_of(lax.rem(o + outer - t, outer), 1 - m, k)
        rwait(block)
        sends.append(rcopy(block, mate, sem, False))
        sends[-1].start()
        sem += 1
    @pl.when(home != x)
    def _():
        def take(block, carry):
            lwait(block)
            return carry

        lax.fori_loop(0, rows, take, 0)

    lf[...] = lbuf[...].astype(F32).reshape(rg * tr, lanes)
    place = (
        lax.broadcasted_iota(jnp.int32, (rg, total), 1) // PACK
        == lax.broadcasted_iota(jnp.int32, (rg, total), 0)
    ).astype(F32).astype(BF16)
    pick = lax.rem(
        lax.broadcasted_iota(jnp.int32, (lanes, total), 1), PACK
    ) == lax.broadcasted_iota(jnp.int32, (lanes, total), 0) // ch
    for i in range(tr):
        y = contract(lf[pl.ds(i, rg, stride=tr), :].astype(BF16), place, 0, 0)
        y = jnp.where(pick, y, 0.0)
        acc = y[0:ch]
        for q in range(1, PACK):
            acc = acc + y[q * ch : (q + 1) * ch]
        lmat[i * ch : (i + 1) * ch, :] = acc.astype(BF16)

    @pl.when(home != x)
    def _():
        def take(block, carry):
            pltpu.make_async_copy(rsend.at[ch], vbuf.at[block], vs_recv.at[block]).wait()
            return carry

        lax.fori_loop(0, rows, take, 0)

    for q in range(0, ch * ch, tc):
        w2t[:, q : q + tc] = pf_dc[q : q + tc, :].T.astype(BF16)
    own_r.wait()
    for t in range(outer):
        for mm in range(2):
            rwait(row_of(lax.rem(o + outer - t, outer), mm, 1 - k))

    @pl.when(home == x)
    def _():
        vbuf[...] = rbuf[:, ch]

    v_left = vbuf[...].astype(F32).reshape(total, tc).astype(BF16)
    v_right = rbuf[:, ch].astype(F32).reshape(total, tc).astype(BF16)
    cnts[...] = contract(v_left, v_right, 0, 0)
    inv = 1.0 / jnp.maximum(cnts[pl.ds(pl.multiple_of(mine * tr, tr), tr), :], 1.0)

    def slab(d):
        return rbuf[:, d].astype(F32).reshape(total, tc).astype(BF16)

    def outer_step(h, carry):
        rd = jnp.concatenate([slab(2 * h), slab(2 * h + 1)], axis=1)
        a = jnp.dot(lmat[...], rd, preferred_element_type=F32)
        for q in range(2):
            part = a[:, q * tc : (q + 1) * tc].reshape(tr, ch, tc) * inv[:, None, :]
            at = pl.multiple_of((2 * h + q) * ch, ch)
            acts[:, pl.ds(at, ch), :] = part.astype(BF16)
        return carry

    lax.fori_loop(0, ch // 2, outer_step, 0, unroll=2)
    load_contact.wait()

    def mask_of(g):
        return jnp.concatenate(
            [cols_live * amino[r * tr + g * wide + i].astype(F32) for i in range(wide)], axis=1
        )

    def panel_of(weight, pn, g):
        raw = contract(weight[...], pn, 0, 0)
        val = raw[:zc] * jax.nn.sigmoid(raw[zc:]) * mask_of(g)
        for i in range(wide):
            psc[pl.ds(g * wide + i, zc, stride=tr), :] = val[:, i * tc : (i + 1) * tc]

    for g in range(tr // wide):
        base = g * wide
        u = jnp.dot(
            w2t[...],
            jnp.concatenate([acts[base + i] for i in range(wide)], axis=1),
            preferred_element_type=F32,
        )
        f = jnp.concatenate([contact[base + i].T for i in range(wide)], axis=1) + u
        first[g] = f
        pn = normalise(f, 0).astype(BF16)
        pns[g] = pn
        panel_of(es, pn, g)
    lp[...] = psc[...].reshape(zc, tr, tc).astype(BF16)

    def tile(ref, rr, xx):
        return ref.at[
            pl.ds(pl.multiple_of(rr * tr, tr), tr), pl.ds(pl.multiple_of(xx * tc, tc), tc)
        ]

    def left_copy(t):
        other, rr, xx = peer(t)
        return pltpu.make_async_remote_copy(
            src_ref=lp.at[pl.ds(other * own, own)],
            dst_ref=lfull.at[
                :, pl.ds(pl.multiple_of(r * tr, tr), tr), pl.ds(pl.multiple_of(x * tc, tc), tc)
            ],
            send_sem=pl_send.at[0],
            recv_sem=pl_recv.at[0],
            device_id={"rows": rr, "cols": xx},
            device_id_type=MESH,
        )

    def right_copy(c, t):
        other, rr, xx = peer(t)
        return pltpu.make_async_remote_copy(
            src_ref=rp.at[other * own + c],
            dst_ref=tile(rfull.at[c], r, x),
            send_sem=pr_send.at[c],
            recv_sem=pr_recv.at[c],
            device_id={"rows": rr, "cols": xx},
            device_id_type=MESH,
        )

    def back_copy(c, t):
        _, rr, xx = peer(t)
        return pltpu.make_async_remote_copy(
            src_ref=tile(prod.at[c], rr, xx),
            dst_ref=pbuf.at[me * own + c],
            send_sem=pb_send.at[c],
            recv_sem=pb_recv.at[c],
            device_id={"rows": rr, "cols": xx},
            device_id_type=MESH,
        )

    def each(fn):
        def step(t, carry):
            fn(t)
            return carry

        lax.fori_loop(1, n, step, 0)

    each(lambda t: left_copy(t).start())
    own_l = pltpu.make_async_copy(
        lp.at[pl.ds(me * own, own)],
        lfull.at[:, pl.ds(pl.multiple_of(r * tr, tr), tr), pl.ds(pl.multiple_of(x * tc, tc), tc)],
        local.at[0],
    )
    own_l.start()
    for g in range(tr // wide):
        panel_of(et, pns[g], g)
    rp[...] = psc[...].reshape(zc, tr, tc).astype(BF16)
    for c in range(min(2, own)):
        each(lambda t: right_copy(c, t).start())
    own_p = []
    for c in range(own):
        own_p.append(
            pltpu.make_async_copy(rp.at[me * own + c], tile(rfull.at[c], r, x), local.at[5 + c])
        )
        own_p[-1].start()
    for g in range(tr // wide):
        gate[g] = jax.nn.sigmoid(contract(efs[...], pns[g], 0, 0))
    own_l.wait()

    def take_all(sem, tiles):
        pltpu.make_async_copy(lp.at[pl.ds(0, tiles)], pbuf.at[pl.ds(0, tiles)], sem).wait()

    take_all(pl_recv.at[0], (n - 1) * own)
    own_b = []
    for c in range(own):
        own_p[c].wait()
        take_all(pr_recv.at[c], n - 1)
        prod[c] = contract(lfull[c], rfull[c], 1, 1).astype(BF16)
        if c + 2 < own:
            each(lambda t: right_copy(c + 2, t).start())
        each(lambda t: back_copy(c, t).start())
        own_b.append(
            pltpu.make_async_copy(
                tile(prod.at[c], r, x), pbuf.at[me * own + c], local.at[5 + own + c]
            )
        )
        own_b[-1].start()

    for s in sends:
        s.wait_send()

    def lsent(t, carry):
        @pl.when(x * rpc + t != r)
        def _():
            lcopy(t).wait_send()

        for step in range(1, cols):
            vcopy(t, step).wait_send()
        return carry

    lax.fori_loop(0, rpc, lsent, 0)

    @pl.when(home == x)
    def _():
        def sent(block, carry):
            for step in range(1, cols):
                hand(block, step).wait_send()
            return carry

        lax.fori_loop(0, rows, sent, 0)

    take_all(pl_send.at[0], (n - 1) * own)
    for c in range(own):
        take_all(pr_send.at[c], n - 1)
    for c in range(own):
        own_b[c].wait()
        take_all(pb_recv.at[c], n - 1)

    psc[...] = normalise(pbuf[...].astype(F32), 0).reshape(zc * tr, tc)
    for g in range(tr // wide):
        mixed = jnp.concatenate(
            [psc[pl.ds(g * wide + i, zc, stride=tr), :].astype(BF16) for i in range(wide)], axis=1
        )
        second = first[g] + gate[g] * contract(ef[...], mixed, 0, 0)
        tn = normalise(second, 0).astype(BF16)
        hidden = jax.nn.relu(contract(fe[...], tn, 0, 0)).astype(BF16)
        res = second + contract(fs[...], hidden, 0, 0)
        for i in range(wide):
            out[g * wide + i] = res[:, i * tc : (i + 1) * tc].T
    for c in range(own):
        take_all(pb_send.at[c], n - 1)


def on_device(fam, keep, amino, contact, wl, wr, pf, es, et, efs, ef, fe, fs):
    rows = lax.axis_size("rows")
    cols = lax.axis_size("cols")
    ns, tc, _ = fam.shape
    tr, _, z = contact.shape
    ch = wl.shape[1]
    zc = es.shape[1] // 2
    groups = ns // PACK
    lanes = PACK * ch
    n = rows * cols
    own = zc // n
    rpc = tc // tr
    total = rows * ns
    wide = 4
    outer = rows // 4
    dma = pltpu.SemaphoreType.DMA
    vmem = pltpu.VMEM
    nsem = outer + 1 + 2 * (outer - 1) + outer
    full = (own, rows * tr, cols * tc)
    return pl.pallas_call(
        functools.partial(fused_kernel, rows, cols, (ns, tc, tr, ch, wide)),
        out_shape=jax.ShapeDtypeStruct((tr, tc, z), F32),
        in_specs=[VM, VM, SM, VM, ANY, VM, VM, ANY] + [VM] * 6,
        out_specs=VM,
        scratch_shapes=[
            vmem((ch + 1, ns, tc), BF16),
            vmem((groups, tc, lanes), BF16),
            vmem((ch * ns, tc), F32),
            vmem((rows, ch + 1, ns, tc), BF16),
            vmem((rows, groups, tr, lanes), BF16),
            vmem((rows, ns, tc), BF16),
            vmem((tr, tc, z), F32),
            vmem((ch * ch, z), BF16),
            vmem((ch * ch, z), F32),
            vmem((ch * ch, z), F32),
            vmem((z, ch * ch), BF16),
            vmem((rows * groups * tr, lanes), F32),
            vmem((tr * ch, total), BF16),
            vmem((tc, tc), F32),
            vmem((tr, ch * ch, tc), BF16),
            vmem((zc * tr, tc), F32),
            vmem((zc, tr, tc), BF16),
            vmem((zc, tr, tc), BF16),
            vmem((tr // wide, z, wide * tc), F32),
            vmem((tr // wide, z, wide * tc), F32),
            vmem((tr // wide, z, wide * tc), BF16),
            vmem(full, BF16),
            vmem(full, BF16),
            vmem(full, BF16),
            vmem((zc, tr, tc), BF16),
            dma((nsem,)),
            dma((rows,)),
            dma((rpc,)),
            dma((rows,)),
            dma((rows, cols - 1)),
            dma((rpc, cols - 1)),
            dma((rows,)),
            dma((1,)),
            dma((1,)),
            dma((own,)),
            dma((own,)),
            dma((own,)),
            dma((own,)),
            dma((5 + 2 * own,)),
        ],
        compiler_params=pltpu.CompilerParams(
            vmem_limit_bytes=60 * 1024 * 1024, collective_id=0, has_side_effects=True
        ),
        name="pair_block",
    )(fam, keep, amino, amino.reshape(1, -1), contact, wl.T, wr.T, pf, es, et, efs, ef, fe, fs)


def solution(mesh):
    tile3 = P(("crops", "rows"), "cols", None)
    in_specs = (tile3, P(("crops", "rows"), "cols"), P("crops"), tile3) + (P(),) * 9
    return jax.shard_map(
        on_device, mesh=mesh, in_specs=in_specs, out_specs=tile3, check_vma=False
    )
```
